32 devices in a mesh: lon: 8 (over y, x, core), lat: 4 (over z).
Axes of the slice: x: 2, y: 2, z: 4, core: 2. Of those that a mesh axis runs over, the one named last changes fastest.
Arguments:
- fields: float32 [5, 1, 128, 11520], P(None, None, 'lat', 'lon'), may hold values from -6 to 6
- frac_x: float32 [2, 1, 128], replicated, may hold values from 0.05 to 0.95
- frac_y: float32 [2, 1, 128], replicated, may hold values from 0.05 to 0.9
- shift_cells: int32 [2, 1, 128], replicated, may hold values from -5760 to 5759, as said below
- polar_mask: int32 [128], replicated, may hold values from 0 to 1, as said below
Outputs:
- fields_out: float32 [5, 1, 128, 11520], P(None, None, 'lat', 'lon')
The draws below stay inside these ranges and needn't reach their ends.
Inputs may be any that keep to these rules, and one draw needn't show every extreme that they name: `shift_cells`: outside the first and last 32 rows every count lies in -2 .. 1, and both -2 and 1 occur there. `polar_mask`: nonzero only in the first and last 32 rows; the first and the last row are 1.
All inputs are finite; a program needn't handle non-finite values.
Results may differ from the reference program's by a relative error of at most 0.00016.
Values sent between devices are 32-bit elements; how exact they have to be, the bound alone decides.
A program may use at most 64 MiB of HBM per device.

```python
import math
import jax
import jax.numpy as jnp

NFIELD = 5
SUBS = 2
REACH = 4
LEV = 1
CLAT = 32
NLON = 11520
CLON = 1440
NLAT = 128


def draw_shift_cells(key, part):
    key_big = jax.random.fold_in(key, 11)
    key_small = jax.random.fold_in(key, 12)
    shape = (SUBS, LEV, NLAT)
    big = jax.random.randint(key_big, shape, -REACH * CLON, REACH * CLON)
    small = jax.random.randint(key_small, shape, -2, 2)
    rows = jnp.arange(NLAT)
    polar = (rows < CLAT) | (rows >= NLAT - CLAT)
    counts = jnp.where(polar[None, None, :], big, small).astype(jnp.int32)
    counts = counts.at[0, 0, 0].set(REACH * CLON - 1)
    counts = counts.at[1, 0, NLAT - 1].set(-REACH * CLON)
    counts = counts.at[0, 0, CLAT].set(-2)
    counts = counts.at[1, 0, CLAT].set(1)
    return counts


def draw_polar_mask(key, part):
    picks = jax.random.randint(jax.random.fold_in(key, 21), (NLAT,), 0, 4)
    rows = jnp.arange(NLAT)
    polar = (rows < CLAT) | (rows >= NLAT - CLAT)
    marks = jnp.where(polar & (picks > 0), 1, 0)
    marks = marks.at[0].set(1).at[NLAT - 1].set(1)
    return marks.astype(jnp.int32)


def block_levels(own_key, shape, shards, low, high):
    def one(axis_at, parts):
        steps = jax.random.uniform(jax.random.fold_in(jax.random.fold_in(own_key, 6), axis_at), (parts,), jnp.float32, low / len(shards), high / len(shards))
        return jnp.repeat(jnp.exp(steps), shape[axis_at] // parts).reshape((-1,) + (1,) * (len(shape) - axis_at - 1))

    factor_of = one(*shards[0])
    for cut in shards[1:]:
        factor_of = factor_of * one(*cut)
    return factor_of


def gaussian(stream_key, shape, spread, most, pieces=(), kind=jnp.bfloat16):
    array = spread * jax.random.normal(stream_key, shape, jnp.float32)
    if pieces:
        array = array * block_levels(stream_key, shape, pieces, -0.22, 0.18)
    return jnp.clip(array, -most, most).astype(kind)


def setup_inputs(seed: int = 0) -> dict:
    seeds = jax.random.split(jax.random.key(seed), 6)
    return {
        "fields": gaussian(seeds[0], (NFIELD, LEV, NLAT, NLON), 1.0, 6.0, ((2, 4), (3, 8)), jnp.float32),
        "frac_x": jnp.clip(jax.random.uniform(seeds[1], (SUBS, LEV, NLAT), jnp.float32, 0.05, 0.95), 0.05, 0.95),
        "frac_y": jnp.clip(jax.random.uniform(seeds[2], (SUBS, LEV, NLAT), jnp.float32, 0.05, 0.9), 0.05, 0.9),
        "shift_cells": draw_shift_cells(jax.random.fold_in(seeds[5], 71), 0),
        "polar_mask": draw_polar_mask(jax.random.fold_in(seeds[5], 71), 0),
    }


def filter_gain(lat_rows):
    phi = math.pi * (lat_rows.astype(jnp.float32) + 0.5) / NLAT - math.pi / 2
    edge_cos = math.sin(math.pi * (CLAT - 0.5) / NLAT)
    b_val = jnp.cos(phi) / edge_cos
    waves = jnp.arange(NLON // 2 + 1, dtype=jnp.int32).astype(jnp.float32)
    sine = jnp.sin(math.pi * waves / NLON)
    return 1.0 / (1.0 + (sine[None, :] ** 2) / (b_val[:, None] ** 2))


def reference(fields, frac_x, frac_y, shift_cells, polar_mask):
    state = fields
    lon_ids = jnp.arange(NLON, dtype=jnp.int32)
    chosen = jnp.concatenate([jnp.arange(CLAT, dtype=jnp.int32), jnp.arange(NLAT - CLAT, NLAT, dtype=jnp.int32)])
    gain = filter_gain(chosen)
    keep = (polar_mask[chosen] == 1)[None, None, :, None]
    face_ids = jnp.arange(NLAT, dtype=jnp.int32)
    for substep in range(SUBS):
        courant = frac_x[substep][None, :, :, None]
        previous = jnp.roll(state, 1, axis=3)
        edge = state + 0.5 * (1.0 - courant) * (state - previous)
        zonal = state - courant * (edge - jnp.roll(edge, 1, axis=3))
        source = (lon_ids[None, None, :] - shift_cells[substep][:, :, None]) % NLON
        shifted = jax.vmap(lambda block: jnp.take_along_axis(block, source, axis=2))(zonal)
        polar_rows = shifted[:, :, chosen, :]
        spectrum = jnp.fft.rfft(polar_rows, axis=3)
        smoothed = jnp.fft.irfft(spectrum * gain[None, None, :, :], n=NLON, axis=3).astype(jnp.float32)
        polar_rows = jnp.where(keep, smoothed, polar_rows)
        filtered = shifted.at[:, :, chosen, :].set(polar_rows)
        merid = jnp.where(face_ids == 0, jnp.zeros_like(frac_y[substep]), frac_y[substep])[None, :, :, None]
        padded = jnp.pad(filtered, ((0, 0), (0, 0), (2, 0), (0, 0)))
        upper = padded[:, :, 1:NLAT + 1, :]
        lower = padded[:, :, 0:NLAT, :]
        flux = merid * (upper + 0.5 * (1.0 - merid) * (upper - lower))
        flux = jnp.concatenate([flux, jnp.zeros_like(flux[:, :, :1, :])], axis=2)
        state = filtered + flux[:, :, :NLAT, :] - flux[:, :, 1:, :]
    return state
```

```python
import functools
import math

import jax
import jax.numpy as jnp
import numpy as np
from jax import lax
from jax.experimental import pallas as pl
from jax.experimental.pallas import tpu as pltpu
from jax.sharding import PartitionSpec as P

SUBS = 2
LANES = 128
HALO = 2
MESH = pl.DeviceIdType.MESH
VMEM_LIMIT = int(58 * 1024 * 1024)


class Plan:
    def __init__(self, mesh, fields_shape):
        self.blocks = mesh.shape["lon"]
        self.bands = mesh.shape["lat"]
        self.fields, _, self.lat_total, self.lon_total = fields_shape
        self.lat = self.lat_total // self.bands
        self.lon = self.lon_total // self.blocks
        self.cols = -(-self.lon // LANES)
        self.rem = self.lon - LANES * (self.cols - 1)
        self.rows = self.fields * self.lat
        self.own = self.rows // self.blocks
        pitch = self.cols
        while (self.own * pitch) % 8 or (HALO * pitch) % 8:
            pitch += 1
        self.pitch = pitch
        self.slots = self.own + 2 * HALO
        self.group = 4 if self.own % 4 == 0 else self.own
        self.groups = self.own // self.group
        self.unit = 2 if self.own % 2 == 0 else 1
        assert self.rows % self.blocks == 0 and self.own <= self.lat
        assert self.blocks & (self.blocks - 1) == 0 and self.blocks % 8 == 0 and self.lat % 8 == 0
        self.south_to = [
            (f, d)
            for f in range(self.fields)
            for d in sorted({f * self.lat // self.own, (f * self.lat + 1) // self.own})
        ]


def decay_table(plan):
    rows = np.arange(plan.lat_total, dtype=np.float64)
    phi = math.pi * (rows + 0.5) / plan.lat_total - math.pi / 2
    b = np.cos(phi) / math.sin(math.pi * (plan.lat - 0.5) / plan.lat_total)
    log_r = -2.0 * np.arcsinh(b)
    r = np.exp(log_r)
    lines = [np.exp(log_r * 2**k) for k in range(7)]
    lines += [np.exp(log_r * LANES), np.exp(log_r * plan.rem)]
    lines += [(1 - r) / (1 + r), 1 / (1 - np.exp(log_r * plan.lon_total)), log_r]
    lines += [np.exp(log_r * plan.lon * 2**k) for k in range(plan.blocks.bit_length() - 1)]
    table = np.stack(lines).astype(np.float32)
    return np.where(np.abs(table) < 1.2e-38, np.float32(0), table)


def build_weights(table, row, weights, slot):
    i = lax.broadcasted_iota(jnp.int32, (LANES, LANES), 0)
    j = lax.broadcasted_iota(jnp.int32, (LANES, LANES), 1)
    apart = jnp.abs(i - j).astype(jnp.float32)
    full = table[9, row] * jnp.exp(table[11, row] * apart)
    high = full.astype(jnp.bfloat16)
    low = (full - high.astype(jnp.float32)).astype(jnp.bfloat16)
    for k in range(2):
        weights[slot, k * LANES : (k + 1) * LANES, :LANES] = high
        weights[slot, k * LANES : (k + 1) * LANES, LANES:] = low


def row_steps(plan, x, courant, count, marked, power, weights):
    blocks, cols, rem = plan.blocks, plan.cols, plan.rem
    lane = lax.broadcasted_iota(jnp.int32, (blocks, LANES), 1)
    tail = lane < rem
    x = x[:-1] + [jnp.where(tail, x[-1], 0.0)]

    half = 0.5 * (1.0 - courant)
    w0 = 1.0 - courant * (1.0 + half)
    w1 = courant * (1.0 + 2.0 * half)
    w2 = -courant * half
    west = pltpu.roll(x[-1], 1, 0)
    before1 = pltpu.roll(west, LANES + 1 - rem, 1) if rem > 1 else west
    before2 = pltpu.roll(west, LANES + 2 - rem, 1)
    zonal = []
    for c in range(cols):
        one, two = pltpu.roll(x[c], 1, 1), pltpu.roll(x[c], 2, 1)
        zonal.append(
            w0 * x[c]
            + w1 * jnp.where(lane < 1, before1, one)
            + w2 * jnp.where(lane < 2, before2, two)
        )
        before1, before2 = one, two

    count = lax.rem(count + plan.lon_total, plan.lon_total)
    moved = [pltpu.roll(z, lax.div(count, plan.lon), 0) for z in zonal]
    start = plan.lon - lax.rem(count, plan.lon)
    western = [pltpu.roll(m, 1, 0) for m in moved]
    turned = [pltpu.roll(m, rem % LANES, 1) for m in moved]
    window = western[:-1]
    for c in range(cols + 1):
        left = western[-1] if c == 0 else turned[c - 1]
        right = turned[c] if c < cols else left
        window.append(jnp.where(tail, left, right))
    first = jnp.full((blocks, LANES), start, jnp.int32) >> 7
    for k in reversed(range((cols - 1).bit_length())):
        by = 1 << k
        taken = (first & by) == by
        window = [
            jnp.where(taken, window[i + by], window[i]) if i + by < len(window) else window[i]
            for i in range(min(len(window), cols + by))
        ]
    within = start & (LANES - 1)
    window = [pltpu.roll(w, (LANES - within) & (LANES - 1), 1) for w in window]
    keep = lane < LANES - jnp.full((blocks, LANES), within, jnp.int32)
    s = [jnp.where(keep, window[c], window[c + 1]) for c in range(cols)]
    s[-1] = jnp.where(tail, s[-1], 0.0)

    r128, r_rem = power(7), power(8)
    closing, log_r = power(10), power(11)
    lane_f = lane.astype(jnp.float32)
    enter_west = jnp.exp(log_r * (lane_f + 1.0))
    enter_east = jnp.exp(log_r * (LANES - lane_f))
    enter_tail = jnp.exp(log_r * jnp.maximum(rem - lane_f, 0.0))
    stacked = jnp.concatenate(s, axis=0)
    high = stacked.astype(jnp.bfloat16)
    low = (stacked - high.astype(jnp.float32)).astype(jnp.bfloat16)
    product = jnp.dot(
        jnp.concatenate([high, low], axis=1), weights, preferred_element_type=jnp.float32
    )
    product = product[:, :LANES] + product[:, LANES:]
    y = [product[c * blocks : (c + 1) * blocks] for c in range(cols)]

    def spread(column, at):
        return jnp.broadcast_to(column[:, at : at + 1], (blocks, LANES))

    ends = [spread(y[c], LANES - 1 if c < cols - 1 else rem - 1) for c in range(cols)]
    begins = [spread(y[c], 0) for c in range(cols)]

    def closed(total, sign):
        total = pltpu.roll(total, 1 if sign > 0 else blocks - 1, 0)
        for k in range(blocks.bit_length() - 1):
            by = 1 << k
            total = total + power(12 + k) * pltpu.roll(total, by if sign > 0 else blocks - by, 0)
        return total * closing

    total = ends[0]
    for c in range(1, cols):
        total = ends[c] + (r128 if c < cols - 1 else r_rem) * total
    carry = closed(total, 1)
    for c in range(cols):
        y[c] = y[c] + enter_west * carry
        carry = ends[c] + r128 * carry
    total = begins[-1]
    for c in range(cols - 2, -1, -1):
        total = begins[c] + r128 * total
    carry = closed(total, -1)
    for c in range(cols - 1, -1, -1):
        y[c] = y[c] + (enter_tail if c == cols - 1 else enter_east) * carry
        carry = begins[c] + (r_rem if c == cols - 1 else r128) * carry
    filtered = jnp.full((blocks, LANES), marked, jnp.int32) == 1
    return [jnp.where(filtered, y[c], s[c]) for c in range(cols)]


def face_weights(plan, cy, t, row):
    last = plan.lat_total - 1
    c0 = jnp.where(row == 0, 0.0, cy[t, 0, row])
    c1 = jnp.where(row == last, 0.0, cy[t, 0, jnp.minimum(row + 1, last)])
    h0, h1 = 0.5 * (1.0 - c0), 0.5 * (1.0 - c1)
    return 1.0 - c1 * (1.0 + h1), c1 * h1 + c0 * (1.0 + h0), -c0 * h0


def start_all(copies):
    for copy in copies:
        copy.start()


def kernel(
    plan, *refs,
):
    inputs, (x_ref, out_ref), tables, rest = refs[:5], refs[5:7], refs[7:12], refs[12:]
    cx, cy, shift, mask, table = tables
    (x_local, x_sem, table_sem, packed, arrived, held, weights, ready, got, got_south, coef,
    in_send, in_recv, halo_send, halo_recv, south_in_send, south_in_recv,
    out_send, out_recv, own_out, south_out_send, south_out_recv, own_in) = rest
    blocks, pitch, own, cols, lat = plan.blocks, plan.pitch, plan.own, plan.cols, plan.lat
    group, groups, slots = plan.group, plan.groups, plan.slots
    me = lax.axis_index("lon")
    band = lax.axis_index("lat")
    has_north = band < plan.bands - 1
    north = lax.rem(band + 1, plan.bands)

    has_south = band > 0
    barrier = pltpu.get_barrier_semaphore()
    for k in range(1, blocks):
        pl.semaphore_signal(
            barrier,
            inc=1,
            device_id={"lon": lax.rem(me + k, blocks), "lat": band},
            device_id_type=MESH,
        )
    for there, to in ((has_north, north), (has_south, lax.rem(band + plan.bands - 1, plan.bands))):

        @pl.when(there)
        def _():
            for k in range(blocks):
                pl.semaphore_signal(
                    barrier, inc=1, device_id={"lon": jnp.int32(k), "lat": to}, device_id_type=MESH
                )

    def lines(first, count):
        return pl.ds(pl.multiple_of(first * pitch, 8), count * pitch)

    def load(f):
        part = pl.ds(f * lat, lat)
        return pltpu.make_async_copy(x_ref.at[part], x_local.at[part], x_sem.at[f])

    start_all([load(f) for f in range(plan.fields)])
    table_copies = [
        pltpu.make_async_copy(source, to, table_sem.at[i])
        for i, (source, to) in enumerate(zip(inputs, tables))
    ]
    start_all(table_copies)
    packed[0 : HALO * pitch, :] = jnp.zeros((HALO * pitch, LANES), jnp.float32)

    def fill(part, none):
        for c in range(cols):
            width = LANES if c < cols - 1 else plan.rem
            v = x_local[pl.ds(pl.multiple_of(part * 8, 8), 8), c * LANES : c * LANES + width]
            if width < LANES:
                v = jnp.concatenate([v, jnp.zeros((8, LANES - width), jnp.float32)], axis=1)
            packed[pl.ds((part * 8 + HALO) * pitch + c, 8, stride=pitch), :] = v
        return none

    for f in range(plan.fields):
        load(f).wait()
        lax.fori_loop(f * (lat // 8), (f + 1) * (lat // 8), fill, 0)

    bands_met = jnp.where(has_north, 1, 0) + jnp.where(has_south, 1, 0)
    pl.semaphore_wait(barrier, blocks - 1 + blocks * bands_met)

    def peer(k):
        return lax.rem(me + k, blocks)

    def halo_in(k):
        return pltpu.make_async_remote_copy(
            src_ref=packed.at[lines(peer(k) * own, HALO)],
            dst_ref=arrived.at[lines(me * slots, HALO)],
            send_sem=halo_send.at[k],
            recv_sem=halo_recv.at[k],
            device_id={"lon": peer(k), "lat": band},
            device_id_type=MESH,
        )

    def group_in(k, g):
        return pltpu.make_async_remote_copy(
            src_ref=packed.at[lines(peer(k) * own + HALO + g * group, group)],
            dst_ref=arrived.at[lines(me * slots + HALO + g * group, group)],
            send_sem=in_send.at[k, g],
            recv_sem=in_recv.at[k, g],
            device_id={"lon": peer(k), "lat": band},
            device_id_type=MESH,
        )

    def south_in(i):
        f, d = plan.south_to[i]
        return pltpu.make_async_remote_copy(
            src_ref=packed.at[lines(HALO + f * lat + lat - HALO, HALO)],
            dst_ref=arrived.at[lines(me * slots + own + HALO, HALO)],
            send_sem=south_in_send.at[i],
            recv_sem=south_in_recv.at[me],
            device_id={"lon": jnp.int32(d), "lat": north},
            device_id_type=MESH,
        )

    local = pltpu.make_async_copy(
        packed.at[lines(me * own, own + HALO)], arrived.at[lines(me * slots, own + HALO)], own_in
    )
    local.start()
    start_all([halo_in(k) for k in range(1, blocks)])

    @pl.when(has_north)
    def _():
        start_all([south_in(i) for i in range(len(plan.south_to))])

    for g in range(groups):
        start_all([group_in(k, g) for k in range(1, blocks)])

    for copy in table_copies:
        copy.wait()

    def place(slot):
        flat = me * own + slot - HALO
        south = slot >= own + HALO
        row = jnp.where(south, slot - (own + 2 * HALO), lax.rem(flat + lat, lat))
        return south, jnp.maximum(band * lat + row, 0)

    def build(slot, none):
        build_weights(table, place(slot)[1], weights, slot)
        return none

    lax.fori_loop(0, slots, build, 0)
    for j in range(lat):
        for i, weight in enumerate(face_weights(plan, cy, SUBS - 1, band * lat + j)):
            coef[i, j : j + 1, :] = jnp.full((1, LANES), weight, jnp.float32)

    def steps(x, t, row, slot):
        return row_steps(
            plan,
            x,
            cx[t, 0, row],
            shift[t, 0, row],
            mask[row],
            lambda i: table[i, row],
            weights[slot],
        )

    def first_pass(slot):
        south, row = place(slot)
        x = [arrived[pl.ds(slot * pitch + c, blocks, stride=slots * pitch), :] for c in range(cols)]
        y = steps(x, 0, row, slot)
        outside = jnp.logical_and(south, band == 0)
        for c in range(cols):
            held[slot, :, c * LANES : (c + 1) * LANES] = jnp.where(outside, 0.0, y[c])

    def second_pass(m):
        j = lax.rem(me * own + m, lat)
        row = band * lat + j
        s0 = m + HALO
        s1 = jnp.where(j == 0, own + 3, s0 - 1)
        s2 = jnp.where(j == 0, own + 2, jnp.where(j == 1, own + 3, s0 - 2))
        a0, a1, a2 = face_weights(plan, cy, 0, row)
        x = []
        for c in range(cols):
            at = slice(c * LANES, (c + 1) * LANES)
            x.append(a0 * held[s0, :, at] + a1 * held[s1, :, at] + a2 * held[s2, :, at])
        y = steps(x, 1, row, s0)
        for c in range(cols):
            ready[pl.ds(m * pitch + c, blocks, stride=own * pitch), :] = y[c]

    def loop(count, each):
        width = 2 if count % 2 == 0 else 1

        def step(i, none):
            for part in range(width):
                each(i * width + part)
            return none

        lax.fori_loop(0, count // width, step, 0)

    def own_back(g):
        return pltpu.make_async_copy(
            ready.at[lines(me * own + g * group, group)],
            got.at[lines(me * own + g * group, group)],
            own_out.at[g],
        )

    def group_back(k, g):
        return pltpu.make_async_remote_copy(
            src_ref=ready.at[lines(peer(k) * own + g * group, group)],
            dst_ref=got.at[lines(me * own + g * group, group)],
            send_sem=out_send.at[k, g],
            recv_sem=out_recv.at[k, g],
            device_id={"lon": peer(k), "lat": band},
            device_id_type=MESH,
        )

    pieces = [(f, part) for f in range(plan.fields) for part in range(HALO // plan.unit)]

    def piece_row(i):
        f, part = pieces[i]
        return f * lat + lat - HALO + part * plan.unit

    def south_back(i, to):
        f, part = pieces[i]
        inside = piece_row(i) % own
        return pltpu.make_async_remote_copy(
            src_ref=ready.at[lines(to * own + inside, plan.unit)],
            dst_ref=got_south.at[lines(f * HALO + part * plan.unit, plan.unit)],
            send_sem=south_out_send.at[i, to],
            recv_sem=south_out_recv.at[i],
            device_id={"lon": jnp.int32(to), "lat": north},
            device_id_type=MESH,
        )

    def sends_south(i):
        return jnp.logical_and(has_north, me == piece_row(i) // own)

    local.wait()
    for k in range(1, blocks):
        halo_in(k).wait_recv()
    for d in sorted({d for _, d in plan.south_to}):

        @pl.when(jnp.logical_and(band > 0, me == d))
        def _():
            for source in range(blocks):
                pltpu.make_async_remote_copy(
                    src_ref=packed.at[lines(0, HALO)],
                    dst_ref=arrived.at[lines(source * slots + own + HALO, HALO)],
                    send_sem=south_in_send.at[0],
                    recv_sem=south_in_recv.at[source],
                    device_id={"lon": me, "lat": lax.rem(band + plan.bands - 1, plan.bands)},
                    device_id_type=MESH,
                ).wait_recv()

    loop(2 * HALO, lambda i: first_pass(jnp.where(i < HALO, i, i + own)))

    def one_group(g, none):
        for k in range(1, blocks):
            group_in(k, g).wait_recv()
        loop(group, lambda i: first_pass(HALO + g * group + i))
        loop(group, lambda i: second_pass(g * group + i))
        own_back(g).start()
        start_all([group_back(k, g) for k in range(1, blocks)])
        for i in range(len(pieces)):

            @pl.when(jnp.logical_and(sends_south(i), g == piece_row(i) % own // group))
            def _():
                start_all([south_back(i, to) for to in range(blocks)])

        return none

    lax.fori_loop(0, groups, one_group, 0)

    for k in range(1, blocks):
        halo_in(k).wait_send()
        for g in range(groups):
            group_in(k, g).wait_send()

    @pl.when(has_north)
    def _():
        for i in range(len(plan.south_to)):
            south_in(i).wait_send()

    for g in range(groups):
        own_back(g).wait()
        for k in range(1, blocks):
            group_back(k, g).wait()
    for i in range(len(pieces)):

        @pl.when(sends_south(i))
        def _():
            for to in range(blocks):
                south_back(i, to).wait_send()

    @pl.when(band > 0)
    def _():
        for i in range(len(pieces)):
            south_back(i, 0).wait_recv()

    @pl.when(band == 0)
    def _():
        got_south[...] = jnp.zeros_like(got_south)

    sub = lax.broadcasted_iota(jnp.int32, (8, LANES), 0)

    def one_field(f, none):
        for g in range(lat // 8):
            a0, a1, a2 = (coef[i, g * 8 : g * 8 + 8, :] for i in range(3))
            for c in range(cols):
                base = (f * lat + g * 8) * pitch + c
                x0 = got[pl.ds(base, 8, stride=pitch), :]
                if g:
                    x1 = got[pl.ds(base - pitch, 8, stride=pitch), :]
                    x2 = got[pl.ds(base - 2 * pitch, 8, stride=pitch), :]
                else:
                    south2 = got_south[pl.ds(f * HALO * pitch + c, 1), :]
                    south1 = got_south[pl.ds((f * HALO + 1) * pitch + c, 1), :]
                    x1 = jnp.where(sub == 0, south1, pltpu.roll(x0, 1, 0))
                    x2 = jnp.where(
                        sub == 0, south2, jnp.where(sub == 1, south1, pltpu.roll(x0, 2, 0))
                    )
                v = a0 * x0 + a1 * x1 + a2 * x2
                width = LANES if c < cols - 1 else plan.rem
                out_ref[f, 0, g * 8 : g * 8 + 8, c * LANES : c * LANES + width] = v[:, :width]
        return none

    lax.fori_loop(0, plan.fields, one_field, 0)


def body(plan, fields, frac_x, frac_y, shift_cells, polar_mask):
    blocks, pitch, own, lat = plan.blocks, plan.pitch, plan.own, plan.lat
    vmem = pl.BlockSpec(memory_space=pltpu.VMEM)
    anywhere = pl.BlockSpec(memory_space=pltpu.HBM)
    dma = pltpu.SemaphoreType.DMA
    n_pieces = plan.fields * (HALO // plan.unit)

    def lines(rows):
        return pltpu.VMEM((rows * pitch, LANES), jnp.float32)

    tables = (frac_x, frac_y, shift_cells, polar_mask, jnp.asarray(decay_table(plan)))
    return pl.pallas_call(
        functools.partial(kernel, plan),
        out_shape=pltpu.VMEM(fields.shape, jnp.float32),
        in_specs=[anywhere] * 6,
        out_specs=vmem,
        scratch_shapes=[
            *[pltpu.SMEM(table.shape, table.dtype) for table in tables],
            pltpu.VMEM((plan.rows, plan.lon), jnp.float32),
            dma((plan.fields,)),
            dma((len(tables),)),
            lines(HALO + plan.rows),
            lines(blocks * plan.slots),
            pltpu.VMEM((plan.slots, blocks, plan.cols * LANES), jnp.float32),
            pltpu.VMEM((plan.slots, 2 * LANES, 2 * LANES), jnp.bfloat16),
            lines(blocks * own),
            lines(plan.rows),
            lines(plan.fields * HALO),
            pltpu.VMEM((3, lat, LANES), jnp.float32),
            dma((blocks, plan.groups)),
            dma((blocks, plan.groups)),
            dma((blocks,)),
            dma((blocks,)),
            dma((len(plan.south_to),)),
            dma((blocks,)),
            dma((blocks, plan.groups)),
            dma((blocks, plan.groups)),
            dma((plan.groups,)),
            dma((n_pieces, blocks)),
            dma((n_pieces,)),
            dma,
        ],
        compiler_params=pltpu.CompilerParams(
            collective_id=0, has_side_effects=True, vmem_limit_bytes=VMEM_LIMIT
        ),
        name="transport",
    )(
        *tables,
        fields.reshape(plan.rows, plan.lon),
    )


def solution(mesh):
    def whole(fields, frac_x, frac_y, shift_cells, polar_mask):
        return jax.shard_map(
            functools.partial(body, Plan(mesh, fields.shape)),
            mesh=mesh,
            in_specs=(P(None, None, "lat", "lon"), P(), P(), P(), P()),
            out_specs=P(None, None, "lat", "lon"),
            check_vma=False,
        )(fields, frac_x, frac_y, shift_cells, polar_mask)

    return whole
```

```python
import functools
import math

import jax
import jax.numpy as jnp
import numpy as np
from jax import lax
from jax.experimental import pallas as pl
from jax.experimental.pallas import tpu as pltpu
from jax.sharding import PartitionSpec as P

SUBS = 2
LANES = 128
HALO = 2
MESH = pl.DeviceIdType.MESH
HELP = (1, 5)
TAPS = 5
VMEM_LIMIT = int(58 * 1024 * 1024)


class Plan:
    def __init__(self, mesh, fields_shape):
        self.blocks = mesh.shape["lon"]
        self.bands = mesh.shape["lat"]
        self.fields, _, self.lat_total, self.lon_total = fields_shape
        self.lat = self.lat_total // self.bands
        self.lon = self.lon_total // self.blocks
        self.cols = -(-self.lon // LANES)
        self.rem = self.lon - LANES * (self.cols - 1)
        self.rows = self.fields * self.lat
        per = self.rows // self.blocks
        self.own_h = per * HELP[0] // HELP[1]
        self.own_a = per - self.own_h
        self.joint = 2 if self.own_h % 2 == 0 and self.own_a % 2 == 0 else 1
        self.unit_a = 2 * self.joint if self.own_a % (2 * self.joint) == 0 else self.joint
        self.unit_h = self.joint
        self.groups_a = self.own_a // self.unit_a
        self.groups_h = self.own_h // self.unit_h
        self.base_h = self.blocks * self.own_a
        pitch = self.cols
        while (self.joint * pitch) % 8:
            pitch += 1
        self.pitch = pitch
        self.ext = -(-(self.cols + 1) // 8) * 8
        self.slots = self.own_a + 2 * HALO
        self.tiles = self.lat // 8
        assert self.rows % self.blocks == 0 and self.own_a <= self.lat and self.bands >= 4
        assert 1 <= self.own_h <= self.own_a and self.lat % 8 == 0
        assert self.blocks & (self.blocks - 1) == 0 and self.blocks % 8 == 0
        assert HALO * SUBS + SUBS <= self.rem <= LANES - 2 * SUBS
        self.south_to = []
        for f in range(self.fields):
            for at in sorted({self.host(f * self.lat), self.host(f * self.lat + 1)}):
                self.south_to.append((f, *at))
        self.pieces = [(f, part) for f in range(self.fields) for part in range(HALO // self.joint)]

    def host(self, flat):
        if flat < self.base_h:
            return 0, flat // self.own_a
        return 1, (flat - self.base_h) // self.own_h

    def piece(self, i):
        f, part = self.pieces[i]
        flat = f * self.lat + self.lat - HALO + part * self.joint
        helper, lon = self.host(flat)
        inside = (flat - self.base_h) % self.own_h if helper else flat % self.own_a
        return helper, lon, inside


def decay_table(plan):
    rows = np.arange(plan.lat_total, dtype=np.float64)
    phi = math.pi * (rows + 0.5) / plan.lat_total - math.pi / 2
    b = np.cos(phi) / math.sin(math.pi * (plan.lat - 0.5) / plan.lat_total)
    log_r = -2.0 * np.arcsinh(b)
    r = np.exp(log_r)
    lines = [np.exp(log_r * 2**k) for k in range(7)]
    lines += [np.exp(log_r * LANES), np.exp(log_r * plan.rem)]
    lines += [(1 - r) / (1 + r), 1 / (1 - np.exp(log_r * plan.lon_total)), log_r]
    lines += [np.exp(log_r * plan.lon * 2**k) for k in range(plan.blocks.bit_length() - 1)]
    table = np.stack(lines).astype(np.float32)
    return np.where(np.abs(table) < 1.2e-38, np.float32(0), table)


def build_weights(table, row, weights, slot):
    i = lax.broadcasted_iota(jnp.int32, (LANES, LANES), 0)
    j = lax.broadcasted_iota(jnp.int32, (LANES, LANES), 1)
    apart = jnp.abs(i - j).astype(jnp.float32)
    full = table[9, row] * jnp.exp(table[11, row] * apart)
    high = full.astype(jnp.bfloat16)
    low = (full - high.astype(jnp.float32)).astype(jnp.bfloat16)
    for k in range(2):
        weights[slot, k * LANES : (k + 1) * LANES, :LANES] = high
        weights[slot, k * LANES : (k + 1) * LANES, LANES:] = low


def row_steps(plan, x, courant, count, marked, power, weights):
    blocks, cols, rem = plan.blocks, plan.cols, plan.rem
    lane = lax.broadcasted_iota(jnp.int32, (blocks, LANES), 1)
    tail = lane < rem
    x = x[:-1] + [jnp.where(tail, x[-1], 0.0)]

    half = 0.5 * (1.0 - courant)
    w0 = 1.0 - courant * (1.0 + half)
    w1 = courant * (1.0 + 2.0 * half)
    w2 = -courant * half
    west = pltpu.roll(x[-1], 1, 0)
    before1 = pltpu.roll(west, LANES + 1 - rem, 1) if rem > 1 else west
    before2 = pltpu.roll(west, LANES + 2 - rem, 1)
    zonal = []
    for c in range(cols):
        one, two = pltpu.roll(x[c], 1, 1), pltpu.roll(x[c], 2, 1)
        zonal.append(
            w0 * x[c]
            + w1 * jnp.where(lane < 1, before1, one)
            + w2 * jnp.where(lane < 2, before2, two)
        )
        before1, before2 = one, two

    count = lax.rem(count + plan.lon_total, plan.lon_total)
    moved = [pltpu.roll(z, lax.div(count, plan.lon), 0) for z in zonal]
    start = plan.lon - lax.rem(count, plan.lon)
    western = [pltpu.roll(m, 1, 0) for m in moved]
    turned = [pltpu.roll(m, rem % LANES, 1) for m in moved]
    window = western[:-1]
    for c in range(cols + 1):
        left = western[-1] if c == 0 else turned[c - 1]
        right = turned[c] if c < cols else left
        window.append(jnp.where(tail, left, right))
    first = jnp.full((blocks, LANES), start, jnp.int32) >> 7
    for k in reversed(range((cols - 1).bit_length())):
        by = 1 << k
        taken = (first & by) == by
        window = [
            jnp.where(taken, window[i + by], window[i]) if i + by < len(window) else window[i]
            for i in range(min(len(window), cols + by))
        ]
    within = start & (LANES - 1)
    window = [pltpu.roll(w, (LANES - within) & (LANES - 1), 1) for w in window]
    keep = lane < LANES - jnp.full((blocks, LANES), within, jnp.int32)
    s = [jnp.where(keep, window[c], window[c + 1]) for c in range(cols)]
    s[-1] = jnp.where(tail, s[-1], 0.0)

    r128, r_rem = power(7), power(8)
    closing, log_r = power(10), power(11)
    lane_f = lane.astype(jnp.float32)
    enter_west = jnp.exp(log_r * (lane_f + 1.0))
    enter_east = jnp.exp(log_r * (LANES - lane_f))
    enter_tail = jnp.exp(log_r * jnp.maximum(rem - lane_f, 0.0))
    stacked = jnp.concatenate(s, axis=0)
    high = stacked.astype(jnp.bfloat16)
    low = (stacked - high.astype(jnp.float32)).astype(jnp.bfloat16)
    product = jnp.dot(
        jnp.concatenate([high, low], axis=1), weights, preferred_element_type=jnp.float32
    )
    product = product[:, :LANES] + product[:, LANES:]
    y = [product[c * blocks : (c + 1) * blocks] for c in range(cols)]

    def spread(column, at):
        return jnp.broadcast_to(column[:, at : at + 1], (blocks, LANES))

    ends = [spread(y[c], LANES - 1 if c < cols - 1 else rem - 1) for c in range(cols)]
    begins = [spread(y[c], 0) for c in range(cols)]

    def closed(total, sign):
        total = pltpu.roll(total, 1 if sign > 0 else blocks - 1, 0)
        for k in range(blocks.bit_length() - 1):
            by = 1 << k
            total = total + power(12 + k) * pltpu.roll(total, by if sign > 0 else blocks - by, 0)
        return total * closing

    total = ends[0]
    for c in range(1, cols):
        total = ends[c] + (r128 if c < cols - 1 else r_rem) * total
    carry = closed(total, 1)
    for c in range(cols):
        y[c] = y[c] + enter_west * carry
        carry = ends[c] + r128 * carry
    total = begins[-1]
    for c in range(cols - 2, -1, -1):
        total = begins[c] + r128 * total
    carry = closed(total, -1)
    for c in range(cols - 1, -1, -1):
        y[c] = y[c] + (enter_tail if c == cols - 1 else enter_east) * carry
        carry = begins[c] + (r_rem if c == cols - 1 else r128) * carry
    filtered = jnp.full((blocks, LANES), marked, jnp.int32) == 1
    return [jnp.where(filtered, y[c], s[c]) for c in range(cols)]


def face_weights(plan, cy, t, row):
    last = plan.lat_total - 1
    c0 = jnp.where(row == 0, 0.0, cy[t, 0, row])
    c1 = jnp.where(row == last, 0.0, cy[t, 0, jnp.minimum(row + 1, last)])
    h0, h1 = 0.5 * (1.0 - c0), 0.5 * (1.0 - c1)
    return 1.0 - c1 * (1.0 + h1), c1 * h1 + c0 * (1.0 + h0), -c0 * h0


def start_all(copies):
    for copy in copies:
        copy.start()


def west_edge(plan, tail):
    return pltpu.roll(tail, LANES - plan.rem, tail.ndim - 1)


def east_edge(plan, first):
    return pltpu.roll(first, plan.rem, first.ndim - 1)


def zonal_taps(tiles, coef, lane, wanted):
    count = len(tiles)
    ahead = {}
    for c in range(max(min(wanted) - 1, 0), max(wanted) + 1):
        x = pltpu.roll(tiles[c], LANES - 2, 1)
        if c + 1 < count:
            x = jnp.where(lane >= LANES - 2, pltpu.roll(tiles[c + 1], LANES - 2, 1), x)
        u = jnp.where(coef[4] > 0.5, x, tiles[c])
        ahead[c] = [u] + [pltpu.roll(u, k, 1) for k in range(1, 4)]
    out = []
    for c in wanted:
        total = coef[0] * ahead[c][0]
        for k in range(1, 4):
            x = ahead[c][k]
            if c > 0:
                x = jnp.where(lane < k, ahead[c - 1][k], x)
            total = total + coef[k] * x
        out.append(total)
    return out


def kernel(plan, *refs):
    inputs, (x_ref, out_ref), tables, rest = refs[:5], refs[5:7], refs[7:15], refs[15:]
    cx, cy, shift, mask, table, cxv, shv, cyv = tables
    (x_local, x_sem, table_sem, packed, arrived, held, weights, ready, got, stage, got_south,
    f1_south, f1_out, ext, edge_out, edge_in, f1, taps, merid,
    in_send, in_recv, halo_send, halo_recv, own_in,
    south_in_send, south_in_recv, ext_send, ext_recv, f1_send, f1_recv, edge_send, edge_recv,
    out_send, out_recv, stage_recv, back_send, back_recv,
    south_out_send, south_out_recv, f2_send, f2_recv) = rest
    blocks, pitch, cols, lat, rem = plan.blocks, plan.pitch, plan.cols, plan.lat, plan.rem
    slots, bands, tiles, joint = plan.slots, plan.bands, plan.tiles, plan.joint
    unit_of = (plan.unit_a, plan.unit_h)
    me = lax.axis_index("lon")
    band = lax.axis_index("lat")
    low = band < 2
    polar = jnp.logical_or(band == 0, band == bands - 1)
    mid = jnp.logical_not(polar)
    helper = jnp.logical_or(band == 1, band == bands - 2)
    worker = jnp.logical_or(polar, helper)
    pole = jnp.where(low, 0, bands - 1)
    help_band = jnp.where(low, 1, bands - 2)
    mate = jnp.where(polar, help_band, pole)
    north_mid = jnp.logical_and(band >= 1, band < bands - 2)
    south_mid = jnp.logical_and(band >= 2, band < bands - 1)
    own = jnp.where(helper, plan.own_h, plan.own_a)
    count = jnp.where(helper, plan.groups_h, plan.groups_a)
    unit = jnp.where(helper, plan.unit_h, plan.unit_a)
    base = jnp.where(helper, plan.base_h, 0)

    def peer(k):
        return lax.rem(me + k, blocks)

    def at(lon, lat_at):
        return {"lon": lon, "lat": lat_at}

    barrier = pltpu.get_barrier_semaphore()

    def greet(lon, lat_at):
        pl.semaphore_signal(barrier, inc=1, device_id=at(lon, lat_at), device_id_type=MESH)

    @pl.when(worker)
    def _():
        for k in range(blocks):
            greet(peer(k), mate)
        for k in range(1, blocks):
            greet(peer(k), band)

    @pl.when(jnp.logical_not(worker))
    def _():
        greet(peer(1), band)
        greet(peer(blocks - 1), band)

    @pl.when(south_mid)
    def _():
        greet(me, band - 1)

    def lines(first, rows, wide=pitch):
        return pl.ds(pl.multiple_of(first * wide, 8), rows * wide)

    def load(f):
        part = pl.ds(f * lat, lat)
        return pltpu.make_async_copy(x_ref.at[part], x_local.at[part], x_sem.at[f])

    start_all([load(f) for f in range(plan.fields)])
    sources = inputs[:5] + (inputs[0], inputs[2], inputs[1])
    table_copies = [
        pltpu.make_async_copy(source, to, table_sem.at[i])
        for i, (source, to) in enumerate(zip(sources, tables))
    ]
    start_all(table_copies)
    packed[0 : HALO * pitch, :] = jnp.zeros((HALO * pitch, LANES), jnp.float32)
    lane = lax.broadcasted_iota(jnp.int32, (8, LANES), 1)
    sub = lax.broadcasted_iota(jnp.int32, (8, LANES), 0)

    def tile_of(part, c):
        width = LANES if c < cols - 1 else rem
        v = x_local[pl.ds(pl.multiple_of(part * 8, 8), 8), c * LANES : c * LANES + width]
        if width < LANES:
            v = jnp.concatenate([v, jnp.zeros((8, LANES - width), jnp.float32)], axis=1)
        return v

    def fill(part, none):
        for c in range(cols):
            packed[pl.ds((part * 8 + HALO) * pitch + c, 8, stride=pitch), :] = tile_of(part, c)
        return none

    def edges(part, none):
        rows = pl.ds(pl.multiple_of(part * 8, 8), 8)
        edge_out[0, rows, :] = west_edge(plan, tile_of(part, cols - 1))
        edge_out[1, rows, :] = east_edge(plan, tile_of(part, 0))
        return none

    for copy in table_copies:
        copy.wait()
    for f in range(plan.fields):
        load(f).wait()

    @pl.when(polar)
    def _():
        lax.fori_loop(0, plan.rows // 8, fill, 0)

    @pl.when(mid)
    def _():
        lax.fori_loop(0, plan.rows // 8, edges, 0, unroll=5)
        lax.fori_loop(0, plan.fields, lambda f, none: fill(f * tiles + tiles - 1, none), 0)

    row_id = lax.broadcasted_iota(jnp.int32, (8, plan.lat_total), 1)
    row_sub = lax.broadcasted_iota(jnp.int32, (8, plan.lat_total), 0)

    def rows_of(vector, first):
        hit = row_id == row_sub + first
        one = jnp.sum(jnp.where(hit, vector, 0.0), axis=1, keepdims=True)
        return jnp.broadcast_to(one, (8, LANES))

    for t in range(SUBS):
        for g in range(tiles):
            first = band * lat + g * 8
            c0 = jnp.where(sub + first == 0, 0.0, rows_of(cyv[t], first))
            c1 = rows_of(cyv[t], first + 1)
            h0, h1 = 0.5 * (1.0 - c0), 0.5 * (1.0 - c1)
            merid[t, g, 0] = 1.0 - c1 * (1.0 + h1)
            merid[t, g, 1] = c1 * h1 + c0 * (1.0 + h0)
            merid[t, g, 2] = -c0 * h0

    @pl.when(mid)
    def _():
        for t in range(SUBS):
            for g in range(tiles):
                first = band * lat + g * 8
                courant = rows_of(cxv[t], first)
                moved = rows_of(shv[t].astype(jnp.float32), first)
                half = 0.5 * (1.0 - courant)
                w0 = 1.0 - courant * (1.0 + half)
                w1 = courant * (1.0 + 2.0 * half)
                w2 = -courant * half
                ahead = moved < -0.5
                still = moved == jnp.where(ahead, -2.0, 0.0)
                taps[t, g, 0] = jnp.where(still, w0, 0.0)
                taps[t, g, 1] = jnp.where(still, w1, w0)
                taps[t, g, 2] = jnp.where(still, w2, w1)
                taps[t, g, 3] = jnp.where(still, 0.0, w2)
                taps[t, g, 4] = jnp.where(ahead, 1.0, 0.0)

    def place(slot):
        flat = base + me * own + slot - HALO
        south = slot >= slots - HALO
        row = jnp.where(south, slot - slots, lax.rem(flat + lat, lat))
        return south, jnp.maximum(pole * lat + row, 0)

    def build(i, none):
        for n in (2 * i, 2 * i + 1) if plan.joint == 2 else (i,):
            slot = jnp.where(n < own + HALO, n, n + slots - 2 * HALO - own)
            build_weights(table, place(slot)[1], weights, slot)
        return none

    @pl.when(polar)
    def _():
        lax.fori_loop(0, (own + 2 * HALO) // plan.joint, build, 0)

    def taps_of(t, i):
        g = lax.rem(i, tiles)
        return [taps[t, g, n] for n in range(TAPS)]

    def put(i, c, v):
        f1[i + i // tiles + 1, c * 8 : c * 8 + 8, :] = v

    def stepped(i, wanted):
        f, g = i // tiles, lax.rem(i, tiles)
        a = [merid[0, g, n] for n in range(3)]
        out = []
        for c in wanted:
            old = f1[i + f, c * 8 : c * 8 + 8, :]
            now = f1[i + f + 1, c * 8 : c * 8 + 8, :]
            one = jnp.where(sub < 1, pltpu.roll(old, 1, 0), pltpu.roll(now, 1, 0))
            two = jnp.where(sub < 2, pltpu.roll(old, 2, 0), pltpu.roll(now, 2, 0))
            out.append(a[0] * now + a[1] * one + a[2] * two)
        return out

    def keep(i, c, v):
        got[pl.ds(i * 8 * pitch + c, 8, stride=pitch), :] = v

    def first_inside(i, none):
        x = [tile_of(i, c) for c in range(cols)]
        for c, v in enumerate(zonal_taps(x, taps_of(0, i), lane, range(cols))):
            put(i, c + 1, v)
        return none

    def second_inside(i, none):
        x = stepped(i, range(1, cols + 1))
        inner = range(1, cols - 1)
        for c, v in zip(inner, zonal_taps(x, taps_of(1, i), lane, inner)):
            keep(i, c, v)
        return none

    def first_edges(i, none):
        rows = pl.ds(pl.multiple_of(i * 8, 8), 8)
        coef = taps_of(0, i)
        x = [edge_in[0, rows, :], tile_of(i, 0), tile_of(i, 1)]
        for c, v in enumerate(zonal_taps(x, coef, lane, range(2))):
            put(i, c, v)
        x = [tile_of(i, cols - 2), tile_of(i, cols - 1)]
        x[1] = jnp.where(lane < rem, x[1], edge_in[1, rows, :])
        put(i, cols, zonal_taps(x, coef, lane, [1])[0])
        return none

    def second_edges(i, none):
        coef = taps_of(1, i)
        keep(i, 0, zonal_taps(stepped(i, range(3)), coef, lane, [1])[0])
        keep(i, cols - 1, zonal_taps(stepped(i, [cols - 1, cols]), coef, lane, [1])[0])
        return none

    def northern(each, unroll):
        def at_tile(i, none):
            return each(i // (tiles - 1) * tiles + lax.rem(i, tiles - 1) + 1, none)

        lax.fori_loop(0, plan.fields * (tiles - 1), at_tile, 0, unroll=unroll)

    @pl.when(mid)
    def _():
        lax.fori_loop(0, plan.rows // 8, first_inside, 0, unroll=2)
        northern(second_inside, 3)

    pl.semaphore_wait(
        barrier,
        jnp.where(worker, 2 * blocks - 1, 2) + jnp.where(north_mid, 1, 0),
    )

    def remote(src, dst, send, recv, lon, lat_at):
        return pltpu.make_async_remote_copy(
            src_ref=src,
            dst_ref=dst,
            send_sem=send,
            recv_sem=recv,
            device_id=at(lon, lat_at),
            device_id_type=MESH,
        )

    def taken(ref, rows, sem, wide=pitch):
        part = ref.at[pl.ds(0, rows * wide)]
        pltpu.make_async_copy(part, part, sem).wait()

    def rows_in(role, k, g):
        own_r, first = (plan.own_h, plan.base_h) if role else (plan.own_a, 0)
        to = peer(k)
        step_rows = unit_of[role]
        return remote(
            packed.at[lines(HALO + first + to * own_r + g * step_rows, step_rows)],
            arrived.at[lines(me * slots + HALO + g * step_rows, step_rows)],
            in_send,
            in_recv.at[g],
            to,
            help_band if role else band,
        )

    def halo_in(role, k):
        own_r, first = (plan.own_h, plan.base_h) if role else (plan.own_a, 0)
        to = peer(k)
        return remote(
            packed.at[lines(first + to * own_r, HALO)],
            arrived.at[lines(me * slots, HALO)],
            halo_send,
            halo_recv,
            to,
            help_band if role else band,
        )

    own_copy = pltpu.make_async_copy(
        packed.at[lines(me * plan.own_a, plan.own_a + HALO)],
        arrived.at[lines(me * slots, plan.own_a + HALO)],
        own_in,
    )

    def start_in():
        for k in range(blocks):
            halo_in(1, k).start()
        for k in range(1, blocks):
            halo_in(0, k).start()
        for g in range(max(plan.groups_a, plan.groups_h)):
            for role in (1, 0):
                if g < (plan.groups_h if role else plan.groups_a):
                    for k in range(0 if role else 1, blocks):
                        rows_in(role, k, g).start()

    @pl.when(polar)
    def _():
        own_copy.start()
        start_in()

    def edge_copy(i):
        to = peer(1 if i == 0 else blocks - 1)
        return remote(edge_out.at[i], edge_in.at[i], edge_send.at[i], edge_recv.at[i], to, band)

    def south_parts(i):
        f, role, d = plan.south_to[i]
        src = packed.at[lines(HALO + f * lat + lat - HALO, HALO)]
        dst = arrived.at[lines(me * slots + slots - HALO, HALO)]
        return role, d, src, dst

    def south_in(i):
        role, d, src, dst = south_parts(i)
        return remote(
            src,
            dst,
            south_in_send.at[i],
            south_in_recv,
            jnp.int32(d),
            jnp.int32(bands - 2 if role else bands - 1),
        )

    def each_south_in(act, local):
        for i in range(len(plan.south_to)):
            role, d, src, dst = south_parts(i)
            if role:

                @pl.when(me != d)
                def _():
                    act(south_in(i))

                @pl.when(me == d)
                def _():
                    if local:
                        pltpu.make_async_copy(src, dst, south_in_recv).start()

            else:
                act(south_in(i))

    @pl.when(mid)
    def _():
        start_all([edge_copy(0), edge_copy(1)])

    @pl.when(band == bands - 2)
    def _():
        each_south_in(lambda copy: copy.start(), True)

    def show_north(f, none):
        for c in range(cols + 1):
            f1_out[pl.ds(f * HALO * plan.ext + c, HALO, stride=plan.ext), :] = f1[
                (f + 1) * (tiles + 1) - 1, c * 8 + 8 - HALO : c * 8 + 8, :
            ]
        return none

    f1_copy = remote(f1_out, f1_south, f1_send, f1_recv, me, band + 1)

    def f2_copy(f):
        return remote(
            got.at[lines(f * lat + lat - HALO, HALO)],
            got_south.at[lines(f * HALO, HALO)],
            f2_send,
            f2_recv,
            me,
            band + 1,
        )

    @pl.when(helper)
    def _():
        lax.fori_loop(0, (own + 2 * HALO) // plan.joint, build, 0)

    @pl.when(mid)
    def _():
        for i in range(2):
            edge_copy(i).wait_recv()
        lax.fori_loop(0, plan.rows // 8, first_edges, 0, unroll=5)
        lax.fori_loop(0, plan.fields, show_north, 0, unroll=True)

        @pl.when(north_mid)
        def _():
            f1_copy.start()

        northern(second_edges, 5)
        start_all([f2_copy(f) for f in range(plan.fields)])

    def steps(x, t, row, slot):
        return row_steps(
            plan,
            x,
            cx[t, 0, row],
            shift[t, 0, row],
            mask[row],
            lambda i: table[i, row],
            weights[slot],
        )

    def first_pass(slot):
        _, row = place(slot)
        x = [arrived[pl.ds(slot * pitch + c, blocks, stride=slots * pitch), :] for c in range(cols)]
        y = steps(x, 0, row, slot)
        for c in range(cols):
            held[slot, :, c * LANES : (c + 1) * LANES] = y[c]

    def second_pass(m):
        j = lax.rem(base + me * own + m, lat)
        row = pole * lat + j
        s0 = m + HALO
        s1 = jnp.where(j == 0, slots - 1, s0 - 1)
        s2 = jnp.where(j == 0, slots - 2, jnp.where(j == 1, slots - 1, s0 - 2))
        a0, a1, a2 = face_weights(plan, cy, 0, row)
        x = []
        for c in range(cols):
            part = slice(c * LANES, (c + 1) * LANES)
            x.append(a0 * held[s0, :, part] + a1 * held[s1, :, part] + a2 * held[s2, :, part])
        y = steps(x, 1, row, s0)
        for c in range(cols):
            ready[pl.ds(m * pitch + c, blocks, stride=plan.own_a * pitch), :] = y[c]

    def hosts(i):
        role, lon, _ = plan.piece(i)
        return jnp.logical_and(me == lon, band == role)

    def ext_parts(i, k):
        f, part = plan.pieces[i]
        src = ext.at[lines((part * blocks + peer(k)) * joint, joint, plan.ext)]
        return src, f1_south.at[lines(f * HALO + part * joint, joint, plan.ext)]

    def f2_parts(i, k):
        f, part = plan.pieces[i]
        src = ready.at[lines(peer(k) * plan.own_a + plan.piece(i)[2], joint)]
        return src, got_south.at[lines(f * HALO + part * joint, joint)]

    def piece_copies(i, parts, send, recv):
        helps = plan.piece(i)[0]
        return [
            remote(*parts(i, k), send.at[i], recv, peer(k), jnp.int32(1))
            for k in range(1 if helps else 0, blocks)
        ]

    def piece_start(i, parts, send, recv):
        start_all(piece_copies(i, parts, send, recv))
        if plan.piece(i)[0]:
            pltpu.make_async_copy(*parts(i, 0), recv).start()

    wide_lane = lax.broadcasted_iota(jnp.int32, (blocks, LANES), 1)

    def widen(i):
        _, _, inside = plan.piece(i)
        part = plan.pieces[i][1]
        for u in range(joint):
            x = [held[inside + u + HALO, :, c * LANES : (c + 1) * LANES] for c in range(cols)]
            west = west_edge(plan, pltpu.roll(x[-1], 1, 0))
            east = east_edge(plan, pltpu.roll(x[0], blocks - 1, 0))
            x[-1] = jnp.where(wide_lane < rem, x[-1], east)
            for c, v in enumerate([west] + x):
                first = (part * blocks * joint + u) * plan.ext + c
                ext[pl.ds(first, blocks, stride=joint * plan.ext), :] = v

    def each_row(g, do):
        def some(i, none):
            for u in range(joint):
                do(g * unit + i * joint + u)
            return none

        lax.fori_loop(0, unit // joint, some, 0)

    def first_group(g):
        @pl.when(polar)
        def _():
            taken(arrived, (blocks - 1) * plan.unit_a, in_recv.at[g])

        @pl.when(helper)
        def _():
            taken(arrived, blocks * plan.unit_h, in_recv.at[g])

        each_row(g, lambda m: first_pass(m + HALO))
        for i in range(len(plan.pieces)):

            @pl.when(jnp.logical_and(hosts(i), g == plan.piece(i)[2] // unit_of[plan.piece(i)[0]]))
            def _():
                widen(i)
                piece_start(i, ext_parts, ext_send, ext_recv)

    is_host = False
    for _, role, d in plan.south_to:
        its = bands - 2 if role else bands - 1
        is_host = jnp.logical_or(is_host, jnp.logical_and(me == d, band == its))

    def others():
        @pl.when(polar)
        def _():
            taken(arrived, (blocks - 1) * HALO, halo_recv)

        @pl.when(helper)
        def _():
            taken(arrived, blocks * HALO, halo_recv)

        @pl.when(is_host)
        def _():
            taken(arrived, blocks * HALO, south_in_recv)

        def two(i, none):
            for u in range(HALO):
                first_pass(i * (slots - HALO) + u)
            return none

        lax.fori_loop(0, 1 + jnp.where(is_host, 1, 0), two, 0)

    def own_back(g):
        rows = plan.unit_a
        part = pl.multiple_of((me * plan.own_a + g * rows) * pitch, 8)
        part = pl.ds(part, rows * pitch)
        return pltpu.make_async_copy(ready.at[part], got.at[part], out_recv)

    def own_stage(g):
        rows = plan.unit_h
        return pltpu.make_async_copy(
            ready.at[lines(me * plan.own_a + g * rows, rows)],
            stage.at[lines(me * plan.own_h + g * rows, rows)],
            stage_recv.at[g],
        )

    def rows_out(k, g):
        rows = plan.unit_a
        return remote(
            ready.at[lines(peer(k) * plan.own_a + g * rows, rows)],
            got.at[lines(me * plan.own_a + g * rows, rows)],
            out_send,
            out_recv,
            peer(k),
            band,
        )

    def rows_stage(k, g):
        rows = plan.unit_h
        return remote(
            ready.at[lines(peer(k) * plan.own_a + g * rows, rows)],
            stage.at[lines(me * plan.own_h + g * rows, rows)],
            out_send,
            stage_recv.at[g],
            peer(k),
            band,
        )

    def relay(g):
        taken(stage, blocks * plan.unit_h, stage_recv.at[g])
        wide = plan.own_h * pitch
        part = pl.ds(pl.multiple_of(g * plan.unit_h * pitch, 8), plan.unit_h * pitch)
        landing = got.at[pl.ds(plan.base_h * pitch, blocks * wide)]
        remote(
            stage.reshape(blocks, wide, LANES).at[:, part, :],
            landing.reshape(blocks, wide, LANES).at[:, part, :],
            back_send,
            back_recv,
            me,
            mate,
        ).start()

    def ship(g):
        @pl.when(polar)
        def _():
            start_all([rows_out(k, g) for k in range(1, blocks)])
            own_back(g).start()

        @pl.when(helper)
        def _():
            start_all([rows_stage(k, g) for k in range(1, blocks)])
            own_stage(g).start()

        for i in range(len(plan.pieces)):

            @pl.when(jnp.logical_and(hosts(i), g == plan.piece(i)[2] // unit_of[plan.piece(i)[0]]))
            def _():
                piece_start(i, f2_parts, south_out_send, south_out_recv)

    @pl.when(polar)
    def _():
        own_copy.wait()

    @pl.when(jnp.logical_and(worker, low))
    def _():
        held[slots - HALO :, :, :] = jnp.zeros((HALO, blocks, cols * LANES), jnp.float32)

    def step(s, none):
        first_group(s)
        each_row(s, second_pass)
        ship(s)

        @pl.when(jnp.logical_and(helper, s > 0))
        def _():
            relay(s - 1)

        return none

    @pl.when(worker)
    def _():
        others()
        lax.fori_loop(0, count, step, 0)

        @pl.when(helper)
        def _():
            relay(plan.groups_h - 1)

    @pl.when(band == 1)
    def _():
        taken(f1_south, plan.fields * HALO, ext_recv, plan.ext)

    @pl.when(south_mid)
    def _():
        remote(f1_out, f1_south, f1_send, f1_recv, me, band + 1).wait_recv()

    @pl.when(mid)
    def _():
        def outer(f, none):
            for c in range(cols + 1):
                f1[f * (tiles + 1), c * 8 + 8 - HALO : c * 8 + 8, :] = f1_south[
                    pl.ds(f * HALO * plan.ext + c, HALO, stride=plan.ext), :
                ]
            i = f * tiles
            x = stepped(i, range(cols + 1))
            for c, v in enumerate(zonal_taps(x, taps_of(1, i), lane, range(1, cols + 1))):
                keep(i, c, v)
            return none

        lax.fori_loop(0, plan.fields, outer, 0)

    @pl.when(polar)
    def _():
        taken(got, plan.base_h, out_recv)
        taken(got, plan.rows - plan.base_h, back_recv)

    @pl.when(band == 0)
    def _():
        got_south[...] = jnp.zeros_like(got_south)

    @pl.when(band == 1)
    def _():
        taken(got_south, plan.fields * HALO, south_out_recv)

    @pl.when(band >= 2)
    def _():
        taken(got_south, plan.fields * HALO, f2_recv)

    def one_field(f, none):
        for g in range(tiles):
            a0, a1, a2 = (merid[SUBS - 1, g, i] for i in range(3))
            for c in range(cols):
                first = (f * lat + g * 8) * pitch + c
                x0 = got[pl.ds(first, 8, stride=pitch), :]
                if g:
                    x1 = got[pl.ds(first - pitch, 8, stride=pitch), :]
                    x2 = got[pl.ds(first - 2 * pitch, 8, stride=pitch), :]
                else:
                    south2 = got_south[pl.ds(f * HALO * pitch + c, 1), :]
                    south1 = got_south[pl.ds((f * HALO + 1) * pitch + c, 1), :]
                    x1 = jnp.where(sub == 0, south1, pltpu.roll(x0, 1, 0))
                    x2 = jnp.where(
                        sub == 0, south2, jnp.where(sub == 1, south1, pltpu.roll(x0, 2, 0))
                    )
                v = a0 * x0 + a1 * x1 + a2 * x2
                width = LANES if c < cols - 1 else rem
                out_ref[f, 0, g * 8 : g * 8 + 8, c * LANES : c * LANES + width] = v[:, :width]
        return none

    lax.fori_loop(0, plan.fields, one_field, 0)

    @pl.when(polar)
    def _():
        taken(packed, (blocks - 1) * plan.own_a + blocks * plan.own_h, in_send)
        taken(ready, (blocks - 1) * plan.own_a, out_send)

        taken(packed, (2 * blocks - 1) * HALO, halo_send)

    @pl.when(helper)
    def _():
        taken(ready, (blocks - 1) * plan.own_h, out_send)
        taken(stage, blocks * plan.own_h, back_send)

    for i in range(len(plan.pieces)):

        @pl.when(hosts(i))
        def _():
            sent = blocks - plan.piece(i)[0]
            taken(ext, sent * joint, ext_send.at[i], plan.ext)
            taken(ready, sent * joint, south_out_send.at[i])

    @pl.when(band == bands - 2)
    def _():
        each_south_in(lambda copy: copy.wait_send(), False)

    @pl.when(north_mid)
    def _():
        f1_copy.wait_send()

    @pl.when(mid)
    def _():
        for i in range(2):
            edge_copy(i).wait_send()
        taken(got, plan.fields * HALO, f2_send)


def body(plan, fields, frac_x, frac_y, shift_cells, polar_mask):
    blocks, pitch = plan.blocks, plan.pitch
    anywhere = pl.BlockSpec(memory_space=pltpu.HBM)
    dma = pltpu.SemaphoreType.DMA
    n_pieces = len(plan.pieces)

    def lines(rows, wide=pitch):
        return pltpu.VMEM((rows * wide, LANES), jnp.float32)

    tables = (frac_x, frac_y, shift_cells, polar_mask, jnp.asarray(decay_table(plan)))
    edge = pltpu.VMEM((2, plan.rows, LANES), jnp.float32)
    return pl.pallas_call(
        functools.partial(kernel, plan),
        out_shape=pltpu.VMEM(fields.shape, jnp.float32),
        in_specs=[anywhere] * 6,
        out_specs=pl.BlockSpec(memory_space=pltpu.VMEM),
        scratch_shapes=[
            *[pltpu.SMEM(table.shape, table.dtype) for table in tables],
            *[pltpu.VMEM(tables[i].shape, tables[i].dtype) for i in (0, 2, 1)],
            pltpu.VMEM((plan.rows, plan.lon), jnp.float32),
            dma((plan.fields,)),
            dma((len(tables) + 3,)),
            lines(HALO + plan.rows),
            lines(blocks * plan.slots),
            pltpu.VMEM((plan.slots, blocks, plan.cols * LANES), jnp.float32),
            pltpu.VMEM((plan.slots, 2 * LANES, 2 * LANES), jnp.bfloat16),
            lines(blocks * plan.own_a),
            lines(plan.rows),
            lines(blocks * plan.own_h),
            lines(plan.fields * HALO),
            lines(plan.fields * HALO, plan.ext),
            lines(plan.fields * HALO, plan.ext),
            lines(blocks * HALO, plan.ext),
            edge,
            edge,
            pltpu.VMEM((plan.fields * (plan.tiles + 1), 8 * (plan.cols + 1), LANES), jnp.float32),
            pltpu.VMEM((SUBS, plan.tiles, TAPS, 8, LANES), jnp.float32),
            pltpu.VMEM((SUBS, plan.tiles, 3, 8, LANES), jnp.float32),
            dma,
            dma((max(plan.groups_a, plan.groups_h),)),
            dma,
            dma,
            dma,
            dma((len(plan.south_to),)),
            dma,
            dma((n_pieces,)),
            dma,
            dma,
            dma,
            dma((2,)),
            dma((2,)),
            dma,
            dma,
            dma((plan.groups_h,)),
            dma,
            dma,
            dma((n_pieces,)),
            dma,
            dma,
            dma,
        ],
        compiler_params=pltpu.CompilerParams(
            collective_id=0, has_side_effects=True, vmem_limit_bytes=VMEM_LIMIT
        ),
        name="transport",
    )(
        *tables,
        fields.reshape(plan.rows, plan.lon),
    )


def solution(mesh):
    def whole(fields, frac_x, frac_y, shift_cells, polar_mask):
        return jax.shard_map(
            functools.partial(body, Plan(mesh, fields.shape)),
            mesh=mesh,
            in_specs=(P(None, None, "lat", "lon"), P(), P(), P(), P()),
            out_specs=P(None, None, "lat", "lon"),
            check_vma=False,
        )(fields, frac_x, frac_y, shift_cells, polar_mask)

    return whole
```

```python
import functools
import math

import jax
import jax.numpy as jnp
import numpy as np
from jax import lax
from jax.experimental import pallas as pl
from jax.experimental.pallas import tpu as pltpu
from jax.sharding import PartitionSpec as P

SUBS = 2
LANES = 128
HALO = 2
MESH = pl.DeviceIdType.MESH
HELP = (3, 10)
RELAY = (1, 3)
TAPS = 5
VMEM_LIMIT = int(58 * 1024 * 1024)


class Plan:
    def __init__(self, mesh, fields_shape):
        self.blocks = mesh.shape["lon"]
        self.bands = mesh.shape["lat"]
        self.fields, _, self.lat_total, self.lon_total = fields_shape
        self.lat = self.lat_total // self.bands
        self.lon = self.lon_total // self.blocks
        self.cols = -(-self.lon // LANES)
        self.rem = self.lon - LANES * (self.cols - 1)
        self.rows = self.fields * self.lat
        per = self.rows // self.blocks
        self.own_h = per * HELP[0] // HELP[1]
        self.own_a = per - self.own_h
        self.joint = 2 if self.own_h % 2 == 0 and self.own_a % 2 == 0 else 1
        self.unit_a = 2 * self.joint if self.own_a % (2 * self.joint) == 0 else self.joint
        self.unit_h = self.joint
        self.groups_a = self.own_a // self.unit_a
        self.groups_h = self.own_h // self.unit_h
        self.base_h = self.blocks * self.own_a
        self.relayed, self.lag = min(RELAY[0], self.groups_h), RELAY[1]
        pitch = self.cols
        while (self.joint * pitch) % 8:
            pitch += 1
        self.pitch = pitch
        self.ext = -(-(self.cols + 1) // 8) * 8
        self.slots = self.own_a + 2 * HALO
        self.tiles = self.lat // 8
        assert self.rows % self.blocks == 0 and self.own_a <= self.lat and self.bands >= 4
        assert 1 <= self.own_h <= self.own_a and self.lat % 8 == 0
        assert self.blocks & (self.blocks - 1) == 0 and self.blocks % 8 == 0
        assert HALO * SUBS + SUBS <= self.rem <= LANES - 2 * SUBS
        self.south_to = []
        for f in range(self.fields):
            for at in sorted({self.host(f * self.lat), self.host(f * self.lat + 1)}):
                self.south_to.append((f, *at))
        self.pieces = [(f, part) for f in range(self.fields) for part in range(HALO // self.joint)]

    def host(self, flat):
        if flat < self.base_h:
            return 0, flat // self.own_a
        return 1, (flat - self.base_h) // self.own_h

    def piece(self, i):
        f, part = self.pieces[i]
        flat = f * self.lat + self.lat - HALO + part * self.joint
        helper, lon = self.host(flat)
        inside = (flat - self.base_h) % self.own_h if helper else flat % self.own_a
        return helper, lon, inside


def decay_table(plan):
    rows = np.arange(plan.lat_total, dtype=np.float64)
    phi = math.pi * (rows + 0.5) / plan.lat_total - math.pi / 2
    b = np.cos(phi) / math.sin(math.pi * (plan.lat - 0.5) / plan.lat_total)
    log_r = -2.0 * np.arcsinh(b)
    r = np.exp(log_r)
    lines = [np.exp(log_r * 2**k) for k in range(7)]
    lines += [np.exp(log_r * LANES), np.exp(log_r * plan.rem)]
    lines += [(1 - r) / (1 + r), 1 / (1 - np.exp(log_r * plan.lon_total)), log_r]
    lines += [np.exp(log_r * plan.lon * 2**k) for k in range(plan.blocks.bit_length() - 1)]
    table = np.stack(lines).astype(np.float32)
    return np.where(np.abs(table) < 1.2e-38, np.float32(0), table)


def build_weights(table, row, weights, slot):
    i = lax.broadcasted_iota(jnp.int32, (LANES, LANES), 0)
    j = lax.broadcasted_iota(jnp.int32, (LANES, LANES), 1)
    apart = jnp.abs(i - j).astype(jnp.float32)
    full = table[9, row] * jnp.exp(table[11, row] * apart)
    high = full.astype(jnp.bfloat16)
    low = (full - high.astype(jnp.float32)).astype(jnp.bfloat16)
    for k in range(2):
        weights[slot, k * LANES : (k + 1) * LANES, :LANES] = high
        weights[slot, k * LANES : (k + 1) * LANES, LANES:] = low


def row_steps(plan, x, courant, count, marked, power, weights):
    blocks, cols, rem = plan.blocks, plan.cols, plan.rem
    lane = lax.broadcasted_iota(jnp.int32, (blocks, LANES), 1)
    tail = lane < rem
    x = x[:-1] + [jnp.where(tail, x[-1], 0.0)]

    half = 0.5 * (1.0 - courant)
    w0 = 1.0 - courant * (1.0 + half)
    w1 = courant * (1.0 + 2.0 * half)
    w2 = -courant * half
    west = pltpu.roll(x[-1], 1, 0)
    before1 = pltpu.roll(west, LANES + 1 - rem, 1) if rem > 1 else west
    before2 = pltpu.roll(west, LANES + 2 - rem, 1)
    zonal = []
    for c in range(cols):
        one, two = pltpu.roll(x[c], 1, 1), pltpu.roll(x[c], 2, 1)
        zonal.append(
            w0 * x[c]
            + w1 * jnp.where(lane < 1, before1, one)
            + w2 * jnp.where(lane < 2, before2, two)
        )
        before1, before2 = one, two

    count = lax.rem(count + plan.lon_total, plan.lon_total)
    moved = [pltpu.roll(z, lax.div(count, plan.lon), 0) for z in zonal]
    start = plan.lon - lax.rem(count, plan.lon)
    western = [pltpu.roll(m, 1, 0) for m in moved]
    turned = [pltpu.roll(m, rem % LANES, 1) for m in moved]
    window = western[:-1]
    for c in range(cols + 1):
        left = western[-1] if c == 0 else turned[c - 1]
        right = turned[c] if c < cols else left
        window.append(jnp.where(tail, left, right))
    first = jnp.full((blocks, LANES), start, jnp.int32) >> 7
    for k in reversed(range((cols - 1).bit_length())):
        by = 1 << k
        taken = (first & by) == by
        window = [
            jnp.where(taken, window[i + by], window[i]) if i + by < len(window) else window[i]
            for i in range(min(len(window), cols + by))
        ]
    within = start & (LANES - 1)
    window = [pltpu.roll(w, (LANES - within) & (LANES - 1), 1) for w in window]
    keep = lane < LANES - jnp.full((blocks, LANES), within, jnp.int32)
    s = [jnp.where(keep, window[c], window[c + 1]) for c in range(cols)]
    s[-1] = jnp.where(tail, s[-1], 0.0)

    r128, r_rem = power(7), power(8)
    closing, log_r = power(10), power(11)
    lane_f = lane.astype(jnp.float32)
    enter_west = jnp.exp(log_r * (lane_f + 1.0))
    enter_east = jnp.exp(log_r * (LANES - lane_f))
    enter_tail = jnp.exp(log_r * jnp.maximum(rem - lane_f, 0.0))
    stacked = jnp.concatenate(s, axis=0)
    high = stacked.astype(jnp.bfloat16)
    low = (stacked - high.astype(jnp.float32)).astype(jnp.bfloat16)
    product = jnp.dot(
        jnp.concatenate([high, low], axis=1), weights, preferred_element_type=jnp.float32
    )
    product = product[:, :LANES] + product[:, LANES:]
    y = [product[c * blocks : (c + 1) * blocks] for c in range(cols)]

    def spread(column, at):
        return jnp.broadcast_to(column[:, at : at + 1], (blocks, LANES))

    ends = [spread(y[c], LANES - 1 if c < cols - 1 else rem - 1) for c in range(cols)]
    begins = [spread(y[c], 0) for c in range(cols)]

    def closed(total, sign):
        total = pltpu.roll(total, 1 if sign > 0 else blocks - 1, 0)
        for k in range(blocks.bit_length() - 1):
            by = 1 << k
            total = total + power(12 + k) * pltpu.roll(total, by if sign > 0 else blocks - by, 0)
        return total * closing

    total = ends[0]
    for c in range(1, cols):
        total = ends[c] + (r128 if c < cols - 1 else r_rem) * total
    carry = closed(total, 1)
    for c in range(cols):
        y[c] = y[c] + enter_west * carry
        carry = ends[c] + r128 * carry
    total = begins[-1]
    for c in range(cols - 2, -1, -1):
        total = begins[c] + r128 * total
    carry = closed(total, -1)
    for c in range(cols - 1, -1, -1):
        y[c] = y[c] + (enter_tail if c == cols - 1 else enter_east) * carry
        carry = begins[c] + (r_rem if c == cols - 1 else r128) * carry
    filtered = jnp.full((blocks, LANES), marked, jnp.int32) == 1
    return [jnp.where(filtered, y[c], s[c]) for c in range(cols)]


def face_weights(plan, cy, t, row):
    last = plan.lat_total - 1
    c0 = jnp.where(row == 0, 0.0, cy[t, 0, row])
    c1 = jnp.where(row == last, 0.0, cy[t, 0, jnp.minimum(row + 1, last)])
    h0, h1 = 0.5 * (1.0 - c0), 0.5 * (1.0 - c1)
    return 1.0 - c1 * (1.0 + h1), c1 * h1 + c0 * (1.0 + h0), -c0 * h0


def start_all(copies):
    for copy in copies:
        copy.start()


def west_edge(plan, tail):
    return pltpu.roll(tail, LANES - plan.rem, tail.ndim - 1)


def east_edge(plan, first):
    return pltpu.roll(first, plan.rem, first.ndim - 1)


def zonal_taps(tiles, coef, lane, wanted):
    count = len(tiles)
    ahead = {}
    for c in range(max(min(wanted) - 1, 0), max(wanted) + 1):
        x = pltpu.roll(tiles[c], LANES - 2, 1)
        if c + 1 < count:
            x = jnp.where(lane >= LANES - 2, pltpu.roll(tiles[c + 1], LANES - 2, 1), x)
        u = jnp.where(coef[4] > 0.5, x, tiles[c])
        ahead[c] = [u] + [pltpu.roll(u, k, 1) for k in range(1, 4)]
    out = []
    for c in wanted:
        total = coef[0] * ahead[c][0]
        for k in range(1, 4):
            x = ahead[c][k]
            if c > 0:
                x = jnp.where(lane < k, ahead[c - 1][k], x)
            total = total + coef[k] * x
        out.append(total)
    return out


def kernel(plan, *refs):
    inputs, (x_ref, out_ref), tables, rest = refs[:5], refs[5:7], refs[7:15], refs[15:]
    cx, cy, shift, mask, table, cxv, shv, cyv = tables
    (x_local, x_sem, table_sem, packed, arrived, held, weights, ready, got, stage, got_south,
    f1_south, f1_out, ext, edge_out, edge_in, f1, taps, merid,
    in_send, in_recv, halo_send, halo_recv, own_in,
    south_in_send, south_in_recv, ext_send, ext_recv, f1_send, f1_recv, edge_send, edge_recv,
    out_send, out_recv, stage_recv, back_send, back_recv,
    south_out_send, south_out_recv, f2_send, f2_recv) = rest
    blocks, pitch, cols, lat, rem = plan.blocks, plan.pitch, plan.cols, plan.lat, plan.rem
    slots, bands, tiles, joint = plan.slots, plan.bands, plan.tiles, plan.joint
    unit_of = (plan.unit_a, plan.unit_h)
    me = lax.axis_index("lon")
    band = lax.axis_index("lat")
    low = band < 2
    polar = jnp.logical_or(band == 0, band == bands - 1)
    mid = jnp.logical_not(polar)
    helper = jnp.logical_or(band == 1, band == bands - 2)
    worker = jnp.logical_or(polar, helper)
    pole = jnp.where(low, 0, bands - 1)
    help_band = jnp.where(low, 1, bands - 2)
    mate = jnp.where(polar, help_band, pole)
    north_mid = jnp.logical_and(band >= 1, band < bands - 2)
    south_mid = jnp.logical_and(band >= 2, band < bands - 1)
    own = jnp.where(helper, plan.own_h, plan.own_a)
    count = jnp.where(helper, plan.groups_h, plan.groups_a)
    unit = jnp.where(helper, plan.unit_h, plan.unit_a)
    base = jnp.where(helper, plan.base_h, 0)

    def peer(k):
        return lax.rem(me + k, blocks)

    def at(lon, lat_at):
        return {"lon": lon, "lat": lat_at}

    barrier = pltpu.get_barrier_semaphore()

    def greet(lon, lat_at):
        pl.semaphore_signal(barrier, inc=1, device_id=at(lon, lat_at), device_id_type=MESH)

    @pl.when(worker)
    def _():
        for k in range(blocks):
            greet(peer(k), mate)
        for k in range(1, blocks):
            greet(peer(k), band)

    @pl.when(jnp.logical_not(worker))
    def _():
        greet(peer(1), band)
        greet(peer(blocks - 1), band)

    @pl.when(south_mid)
    def _():
        greet(me, band - 1)

    def lines(first, rows, wide=pitch):
        return pl.ds(pl.multiple_of(first * wide, 8), rows * wide)

    def load(f):
        part = pl.ds(f * lat, lat)
        return pltpu.make_async_copy(x_ref.at[part], x_local.at[part], x_sem.at[f])

    start_all([load(f) for f in range(plan.fields)])
    sources = inputs[:5] + (inputs[0], inputs[2], inputs[1])
    table_copies = [
        pltpu.make_async_copy(source, to, table_sem.at[i])
        for i, (source, to) in enumerate(zip(sources, tables))
    ]
    start_all(table_copies)
    packed[0 : HALO * pitch, :] = jnp.zeros((HALO * pitch, LANES), jnp.float32)
    lane = lax.broadcasted_iota(jnp.int32, (8, LANES), 1)
    sub = lax.broadcasted_iota(jnp.int32, (8, LANES), 0)

    def tile_of(part, c):
        width = LANES if c < cols - 1 else rem
        v = x_local[pl.ds(pl.multiple_of(part * 8, 8), 8), c * LANES : c * LANES + width]
        if width < LANES:
            v = jnp.concatenate([v, jnp.zeros((8, LANES - width), jnp.float32)], axis=1)
        return v

    def fill(part, none):
        for c in range(cols):
            packed[pl.ds((part * 8 + HALO) * pitch + c, 8, stride=pitch), :] = tile_of(part, c)
        return none

    def edges(part, none):
        rows = pl.ds(pl.multiple_of(part * 8, 8), 8)
        edge_out[0, rows, :] = west_edge(plan, tile_of(part, cols - 1))
        edge_out[1, rows, :] = east_edge(plan, tile_of(part, 0))
        return none

    for copy in table_copies:
        copy.wait()
    for f in range(plan.fields):
        load(f).wait()

    @pl.when(polar)
    def _():
        lax.fori_loop(0, plan.rows // 8, fill, 0)

    @pl.when(mid)
    def _():
        lax.fori_loop(0, plan.rows // 8, edges, 0, unroll=5)
        lax.fori_loop(0, plan.fields, lambda f, none: fill(f * tiles + tiles - 1, none), 0)

    row_id = lax.broadcasted_iota(jnp.int32, (8, plan.lat_total), 1)
    row_sub = lax.broadcasted_iota(jnp.int32, (8, plan.lat_total), 0)

    def rows_of(vector, first):
        hit = row_id == row_sub + first
        one = jnp.sum(jnp.where(hit, vector, 0.0), axis=1, keepdims=True)
        return jnp.broadcast_to(one, (8, LANES))

    for t in range(SUBS):
        for g in range(tiles):
            first = band * lat + g * 8
            c0 = jnp.where(sub + first == 0, 0.0, rows_of(cyv[t], first))
            c1 = rows_of(cyv[t], first + 1)
            h0, h1 = 0.5 * (1.0 - c0), 0.5 * (1.0 - c1)
            merid[t, g, 0] = 1.0 - c1 * (1.0 + h1)
            merid[t, g, 1] = c1 * h1 + c0 * (1.0 + h0)
            merid[t, g, 2] = -c0 * h0

    @pl.when(mid)
    def _():
        for t in range(SUBS):
            for g in range(tiles):
                first = band * lat + g * 8
                courant = rows_of(cxv[t], first)
                moved = rows_of(shv[t].astype(jnp.float32), first)
                half = 0.5 * (1.0 - courant)
                w0 = 1.0 - courant * (1.0 + half)
                w1 = courant * (1.0 + 2.0 * half)
                w2 = -courant * half
                ahead = moved < -0.5
                still = moved == jnp.where(ahead, -2.0, 0.0)
                taps[t, g, 0] = jnp.where(still, w0, 0.0)
                taps[t, g, 1] = jnp.where(still, w1, w0)
                taps[t, g, 2] = jnp.where(still, w2, w1)
                taps[t, g, 3] = jnp.where(still, 0.0, w2)
                taps[t, g, 4] = jnp.where(ahead, 1.0, 0.0)

    def place(slot):
        flat = base + me * own + slot - HALO
        south = slot >= slots - HALO
        row = jnp.where(south, slot - slots, lax.rem(flat + lat, lat))
        return south, jnp.maximum(pole * lat + row, 0)

    def build(i, none):
        for n in (2 * i, 2 * i + 1) if plan.joint == 2 else (i,):
            slot = jnp.where(n < own + HALO, n, n + slots - 2 * HALO - own)
            build_weights(table, place(slot)[1], weights, slot)
        return none

    @pl.when(polar)
    def _():
        lax.fori_loop(0, (own + 2 * HALO) // plan.joint, build, 0)

    def taps_of(t, i):
        g = lax.rem(i, tiles)
        return [taps[t, g, n] for n in range(TAPS)]

    def put(i, c, v):
        f1[i + i // tiles + 1, c * 8 : c * 8 + 8, :] = v

    def stepped(i, wanted):
        f, g = i // tiles, lax.rem(i, tiles)
        a = [merid[0, g, n] for n in range(3)]
        out = []
        for c in wanted:
            old = f1[i + f, c * 8 : c * 8 + 8, :]
            now = f1[i + f + 1, c * 8 : c * 8 + 8, :]
            one = jnp.where(sub < 1, pltpu.roll(old, 1, 0), pltpu.roll(now, 1, 0))
            two = jnp.where(sub < 2, pltpu.roll(old, 2, 0), pltpu.roll(now, 2, 0))
            out.append(a[0] * now + a[1] * one + a[2] * two)
        return out

    def keep(i, c, v):
        got[pl.ds(i * 8 * pitch + c, 8, stride=pitch), :] = v

    def first_inside(i, none):
        x = [tile_of(i, c) for c in range(cols)]
        for c, v in enumerate(zonal_taps(x, taps_of(0, i), lane, range(cols))):
            put(i, c + 1, v)
        return none

    def second_inside(i, none):
        x = stepped(i, range(1, cols + 1))
        inner = range(1, cols - 1)
        for c, v in zip(inner, zonal_taps(x, taps_of(1, i), lane, inner)):
            keep(i, c, v)
        return none

    def first_edges(i, none):
        rows = pl.ds(pl.multiple_of(i * 8, 8), 8)
        coef = taps_of(0, i)
        x = [edge_in[0, rows, :], tile_of(i, 0), tile_of(i, 1)]
        for c, v in enumerate(zonal_taps(x, coef, lane, range(2))):
            put(i, c, v)
        x = [tile_of(i, cols - 2), tile_of(i, cols - 1)]
        x[1] = jnp.where(lane < rem, x[1], edge_in[1, rows, :])
        put(i, cols, zonal_taps(x, coef, lane, [1])[0])
        return none

    def second_edges(i, none):
        coef = taps_of(1, i)
        keep(i, 0, zonal_taps(stepped(i, range(3)), coef, lane, [1])[0])
        keep(i, cols - 1, zonal_taps(stepped(i, [cols - 1, cols]), coef, lane, [1])[0])
        return none

    def northern(each, unroll):
        def at_tile(i, none):
            return each(i // (tiles - 1) * tiles + lax.rem(i, tiles - 1) + 1, none)

        lax.fori_loop(0, plan.fields * (tiles - 1), at_tile, 0, unroll=unroll)

    @pl.when(mid)
    def _():
        lax.fori_loop(0, plan.rows // 8, first_inside, 0, unroll=2)
        northern(second_inside, 3)

    pl.semaphore_wait(
        barrier,
        jnp.where(worker, 2 * blocks - 1, 2) + jnp.where(north_mid, 1, 0),
    )

    def remote(src, dst, send, recv, lon, lat_at):
        return pltpu.make_async_remote_copy(
            src_ref=src,
            dst_ref=dst,
            send_sem=send,
            recv_sem=recv,
            device_id=at(lon, lat_at),
            device_id_type=MESH,
        )

    def taken(ref, rows, sem, wide=pitch):
        part = ref.at[pl.ds(0, rows * wide)]
        pltpu.make_async_copy(part, part, sem).wait()

    def rows_in(role, k, g):
        own_r, first = (plan.own_h, plan.base_h) if role else (plan.own_a, 0)
        to = peer(k)
        step_rows = unit_of[role]
        return remote(
            packed.at[lines(HALO + first + to * own_r + g * step_rows, step_rows)],
            arrived.at[lines(me * slots + HALO + g * step_rows, step_rows)],
            in_send,
            in_recv.at[g],
            to,
            help_band if role else band,
        )

    def halo_in(role, k):
        own_r, first = (plan.own_h, plan.base_h) if role else (plan.own_a, 0)
        to = peer(k)
        return remote(
            packed.at[lines(first + to * own_r, HALO)],
            arrived.at[lines(me * slots, HALO)],
            halo_send,
            halo_recv,
            to,
            help_band if role else band,
        )

    own_copy = pltpu.make_async_copy(
        packed.at[lines(me * plan.own_a, plan.own_a + HALO)],
        arrived.at[lines(me * slots, plan.own_a + HALO)],
        own_in,
    )

    def start_in():
        for k in range(blocks):
            halo_in(1, k).start()
        for k in range(1, blocks):
            halo_in(0, k).start()
        for g in range(max(plan.groups_a, plan.groups_h)):
            for role in (1, 0):
                if g < (plan.groups_h if role else plan.groups_a):
                    for k in range(0 if role else 1, blocks):
                        rows_in(role, k, g).start()

    @pl.when(polar)
    def _():
        own_copy.start()
        start_in()

    def edge_copy(i):
        to = peer(1 if i == 0 else blocks - 1)
        return remote(edge_out.at[i], edge_in.at[i], edge_send.at[i], edge_recv.at[i], to, band)

    def south_parts(i):
        f, role, d = plan.south_to[i]
        src = packed.at[lines(HALO + f * lat + lat - HALO, HALO)]
        dst = arrived.at[lines(me * slots + slots - HALO, HALO)]
        return role, d, src, dst

    def south_in(i):
        role, d, src, dst = south_parts(i)
        return remote(
            src,
            dst,
            south_in_send.at[i],
            south_in_recv,
            jnp.int32(d),
            jnp.int32(bands - 2 if role else bands - 1),
        )

    def each_south_in(act, local):
        for i in range(len(plan.south_to)):
            role, d, src, dst = south_parts(i)
            if role:

                @pl.when(me != d)
                def _():
                    act(south_in(i))

                @pl.when(me == d)
                def _():
                    if local:
                        pltpu.make_async_copy(src, dst, south_in_recv).start()

            else:
                act(south_in(i))

    @pl.when(mid)
    def _():
        start_all([edge_copy(0), edge_copy(1)])

    @pl.when(band == bands - 2)
    def _():
        each_south_in(lambda copy: copy.start(), True)

    def show_north(f, none):
        for c in range(cols + 1):
            f1_out[pl.ds(f * HALO * plan.ext + c, HALO, stride=plan.ext), :] = f1[
                (f + 1) * (tiles + 1) - 1, c * 8 + 8 - HALO : c * 8 + 8, :
            ]
        return none

    f1_copy = remote(f1_out, f1_south, f1_send, f1_recv, me, band + 1)

    def f2_copy(f):
        return remote(
            got.at[lines(f * lat + lat - HALO, HALO)],
            got_south.at[lines(f * HALO, HALO)],
            f2_send,
            f2_recv,
            me,
            band + 1,
        )

    @pl.when(helper)
    def _():
        lax.fori_loop(0, (own + 2 * HALO) // plan.joint, build, 0)

    def close_first():
        for i in range(2):
            edge_copy(i).wait_recv()
        lax.fori_loop(0, plan.rows // 8, first_edges, 0, unroll=5)

        @pl.when(north_mid)
        def _():
            lax.fori_loop(0, plan.fields, show_north, 0, unroll=True)
            f1_copy.start()

    def close_second():
        northern(second_edges, 5)
        start_all([f2_copy(f) for f in range(plan.fields)])

    def steps(x, t, row, slot):
        return row_steps(
            plan,
            x,
            cx[t, 0, row],
            shift[t, 0, row],
            mask[row],
            lambda i: table[i, row],
            weights[slot],
        )

    def first_pass(slot):
        _, row = place(slot)
        x = [arrived[pl.ds(slot * pitch + c, blocks, stride=slots * pitch), :] for c in range(cols)]
        y = steps(x, 0, row, slot)
        for c in range(cols):
            held[slot, :, c * LANES : (c + 1) * LANES] = y[c]

    def second_pass(m):
        j = lax.rem(base + me * own + m, lat)
        row = pole * lat + j
        s0 = m + HALO
        s1 = jnp.where(j == 0, slots - 1, s0 - 1)
        s2 = jnp.where(j == 0, slots - 2, jnp.where(j == 1, slots - 1, s0 - 2))
        a0, a1, a2 = face_weights(plan, cy, 0, row)
        x = []
        for c in range(cols):
            part = slice(c * LANES, (c + 1) * LANES)
            x.append(a0 * held[s0, :, part] + a1 * held[s1, :, part] + a2 * held[s2, :, part])
        y = steps(x, 1, row, s0)
        for c in range(cols):
            ready[pl.ds(m * pitch + c, blocks, stride=plan.own_a * pitch), :] = y[c]

    def hosts(i):
        role, lon, _ = plan.piece(i)
        return jnp.logical_and(me == lon, band == role)

    def ext_parts(i, k):
        f, part = plan.pieces[i]
        src = ext.at[lines((part * blocks + peer(k)) * joint, joint, plan.ext)]
        return src, f1_south.at[lines(f * HALO + part * joint, joint, plan.ext)]

    def f2_parts(i, k):
        f, part = plan.pieces[i]
        src = ready.at[lines(peer(k) * plan.own_a + plan.piece(i)[2], joint)]
        return src, got_south.at[lines(f * HALO + part * joint, joint)]

    def piece_copies(i, parts, send, recv):
        helps = plan.piece(i)[0]
        return [
            remote(*parts(i, k), send.at[i], recv, peer(k), jnp.int32(1))
            for k in range(1 if helps else 0, blocks)
        ]

    def piece_start(i, parts, send, recv):
        start_all(piece_copies(i, parts, send, recv))
        if plan.piece(i)[0]:
            pltpu.make_async_copy(*parts(i, 0), recv).start()

    wide_lane = lax.broadcasted_iota(jnp.int32, (blocks, LANES), 1)

    def widen(i):
        _, _, inside = plan.piece(i)
        part = plan.pieces[i][1]
        for u in range(joint):
            x = [held[inside + u + HALO, :, c * LANES : (c + 1) * LANES] for c in range(cols)]
            west = west_edge(plan, pltpu.roll(x[-1], 1, 0))
            east = east_edge(plan, pltpu.roll(x[0], blocks - 1, 0))
            x[-1] = jnp.where(wide_lane < rem, x[-1], east)
            for c, v in enumerate([west] + x):
                first = (part * blocks * joint + u) * plan.ext + c
                ext[pl.ds(first, blocks, stride=joint * plan.ext), :] = v

    def each_row(g, do):
        def some(i, none):
            for u in range(joint):
                do(g * unit + i * joint + u)
            return none

        lax.fori_loop(0, unit // joint, some, 0)

    def first_group(g):
        @pl.when(polar)
        def _():
            taken(arrived, (blocks - 1) * plan.unit_a, in_recv.at[g])

        @pl.when(helper)
        def _():
            taken(arrived, blocks * plan.unit_h, in_recv.at[g])

        each_row(g, lambda m: first_pass(m + HALO))
        for i in range(len(plan.pieces)):

            @pl.when(jnp.logical_and(hosts(i), g == plan.piece(i)[2] // unit_of[plan.piece(i)[0]]))
            def _():
                widen(i)
                piece_start(i, ext_parts, ext_send, ext_recv)

    is_host = False
    for _, role, d in plan.south_to:
        its = bands - 2 if role else bands - 1
        is_host = jnp.logical_or(is_host, jnp.logical_and(me == d, band == its))

    def others():
        @pl.when(polar)
        def _():
            taken(arrived, (blocks - 1) * HALO, halo_recv)

        @pl.when(helper)
        def _():
            taken(arrived, blocks * HALO, halo_recv)

        @pl.when(is_host)
        def _():
            taken(arrived, blocks * HALO, south_in_recv)

        def two(i, none):
            for u in range(HALO):
                first_pass(i * (slots - HALO) + u)
            return none

        lax.fori_loop(0, 1 + jnp.where(is_host, 1, 0), two, 0)

    def own_back(g):
        rows = plan.unit_a
        part = pl.multiple_of((me * plan.own_a + g * rows) * pitch, 8)
        part = pl.ds(part, rows * pitch)
        return pltpu.make_async_copy(ready.at[part], got.at[part], out_recv)

    def own_stage(g):
        rows = plan.unit_h
        return pltpu.make_async_copy(
            ready.at[lines(me * plan.own_a + g * rows, rows)],
            stage.at[lines(me * plan.own_h + g * rows, rows)],
            stage_recv.at[g],
        )

    def rows_out(k, g):
        rows = plan.unit_a
        return remote(
            ready.at[lines(peer(k) * plan.own_a + g * rows, rows)],
            got.at[lines(me * plan.own_a + g * rows, rows)],
            out_send,
            out_recv,
            peer(k),
            band,
        )

    def rows_home(k, g):
        rows = plan.unit_h
        return remote(
            ready.at[lines(peer(k) * plan.own_a + g * rows, rows)],
            got.at[lines(plan.base_h + me * plan.own_h + g * rows, rows)],
            out_send,
            back_recv,
            peer(k),
            mate,
        )

    def rows_stage(k, g):
        rows = plan.unit_h
        return remote(
            ready.at[lines(peer(k) * plan.own_a + g * rows, rows)],
            stage.at[lines(me * plan.own_h + g * rows, rows)],
            out_send,
            stage_recv.at[g],
            peer(k),
            band,
        )

    def relay(g):
        taken(stage, blocks * plan.unit_h, stage_recv.at[g])
        wide = plan.own_h * pitch
        part = pl.ds(pl.multiple_of(g * plan.unit_h * pitch, 8), plan.unit_h * pitch)
        landing = got.at[pl.ds(plan.base_h * pitch, blocks * wide)]
        remote(
            stage.reshape(blocks, wide, LANES).at[:, part, :],
            landing.reshape(blocks, wide, LANES).at[:, part, :],
            back_send,
            back_recv,
            me,
            mate,
        ).start()

    def ship(g):
        @pl.when(polar)
        def _():
            start_all([rows_out(k, g) for k in range(1, blocks)])
            own_back(g).start()

        @pl.when(helper)
        def _():
            @pl.when(g < plan.relayed)
            def _():
                start_all([rows_stage(k, g) for k in range(1, blocks)])
                own_stage(g).start()

            @pl.when(g >= plan.relayed)
            def _():
                start_all([rows_home(k, g) for k in range(blocks)])

        for i in range(len(plan.pieces)):

            @pl.when(jnp.logical_and(hosts(i), g == plan.piece(i)[2] // unit_of[plan.piece(i)[0]]))
            def _():
                piece_start(i, f2_parts, south_out_send, south_out_recv)

    @pl.when(polar)
    def _():
        own_copy.wait()

    @pl.when(jnp.logical_and(worker, low))
    def _():
        held[slots - HALO :, :, :] = jnp.zeros((HALO, blocks, cols * LANES), jnp.float32)

    def step(s, none):
        first_group(s)
        each_row(s, second_pass)
        ship(s)

        @pl.when(jnp.logical_and(helper, s == 0))
        def _():
            close_first()

        @pl.when(jnp.logical_and(helper, s == min(1, plan.groups_h - 1)))
        def _():
            close_second()

        @pl.when(jnp.logical_and(helper, jnp.logical_and(s >= plan.lag, s < plan.relayed + plan.lag)))
        def _():
            relay(s - plan.lag)

        return none

    if bands > 4:

        @pl.when(jnp.logical_not(worker))
        def _():
            close_first()
            close_second()

    @pl.when(worker)
    def _():
        others()
        lax.fori_loop(0, count, step, 0)

        @pl.when(helper)
        def _():
            for g in range(max(plan.groups_h - plan.lag, 0), plan.relayed):
                relay(g)

    @pl.when(band == 1)
    def _():
        taken(f1_south, plan.fields * HALO, ext_recv, plan.ext)

    @pl.when(south_mid)
    def _():
        remote(f1_out, f1_south, f1_send, f1_recv, me, band + 1).wait_recv()

    @pl.when(mid)
    def _():
        def outer(f, none):
            for c in range(cols + 1):
                f1[f * (tiles + 1), c * 8 + 8 - HALO : c * 8 + 8, :] = f1_south[
                    pl.ds(f * HALO * plan.ext + c, HALO, stride=plan.ext), :
                ]
            i = f * tiles
            x = stepped(i, range(cols + 1))
            for c, v in enumerate(zonal_taps(x, taps_of(1, i), lane, range(1, cols + 1))):
                keep(i, c, v)
            return none

        lax.fori_loop(0, plan.fields, outer, 0)

    @pl.when(polar)
    def _():
        taken(got, plan.base_h, out_recv)

    @pl.when(band == 0)
    def _():
        got_south[...] = jnp.zeros_like(got_south)

    @pl.when(band == 1)
    def _():
        taken(got_south, plan.fields * HALO, south_out_recv)

    @pl.when(band >= 2)
    def _():
        taken(got_south, plan.fields * HALO, f2_recv)

    def one_field(f, none):
        for g in range(tiles):
            a0, a1, a2 = (merid[SUBS - 1, g, i] for i in range(3))
            for c in range(cols):
                first = (f * lat + g * 8) * pitch + c
                x0 = got[pl.ds(first, 8, stride=pitch), :]
                if g:
                    x1 = got[pl.ds(first - pitch, 8, stride=pitch), :]
                    x2 = got[pl.ds(first - 2 * pitch, 8, stride=pitch), :]
                else:
                    south2 = got_south[pl.ds(f * HALO * pitch + c, 1), :]
                    south1 = got_south[pl.ds((f * HALO + 1) * pitch + c, 1), :]
                    x1 = jnp.where(sub == 0, south1, pltpu.roll(x0, 1, 0))
                    x2 = jnp.where(
                        sub == 0, south2, jnp.where(sub == 1, south1, pltpu.roll(x0, 2, 0))
                    )
                v = a0 * x0 + a1 * x1 + a2 * x2
                width = LANES if c < cols - 1 else rem
                out_ref[f, 0, g * 8 : g * 8 + 8, c * LANES : c * LANES + width] = v[:, :width]
        return none

    early = plan.base_h // lat
    lax.fori_loop(0, early, one_field, 0)

    @pl.when(polar)
    def _():
        taken(got, plan.rows - plan.base_h, back_recv)

    lax.fori_loop(early, plan.fields, one_field, 0)

    @pl.when(polar)
    def _():
        taken(packed, (blocks - 1) * plan.own_a + blocks * plan.own_h, in_send)
        taken(ready, (blocks - 1) * plan.own_a, out_send)

        taken(packed, (2 * blocks - 1) * HALO, halo_send)

    @pl.when(helper)
    def _():
        straight = plan.own_h - plan.relayed * plan.unit_h
        taken(ready, (blocks - 1) * plan.own_h + straight, out_send)
        if plan.relayed:
            taken(stage, blocks * plan.relayed * plan.unit_h, back_send)

    for i in range(len(plan.pieces)):

        @pl.when(hosts(i))
        def _():
            sent = blocks - plan.piece(i)[0]
            taken(ext, sent * joint, ext_send.at[i], plan.ext)
            taken(ready, sent * joint, south_out_send.at[i])

    @pl.when(band == bands - 2)
    def _():
        each_south_in(lambda copy: copy.wait_send(), False)

    @pl.when(north_mid)
    def _():
        f1_copy.wait_send()

    @pl.when(mid)
    def _():
        for i in range(2):
            edge_copy(i).wait_send()
        taken(got, plan.fields * HALO, f2_send)


def body(plan, fields, frac_x, frac_y, shift_cells, polar_mask):
    blocks, pitch = plan.blocks, plan.pitch
    anywhere = pl.BlockSpec(memory_space=pltpu.HBM)
    dma = pltpu.SemaphoreType.DMA
    n_pieces = len(plan.pieces)

    def lines(rows, wide=pitch):
        return pltpu.VMEM((rows * wide, LANES), jnp.float32)

    tables = (frac_x, frac_y, shift_cells, polar_mask, jnp.asarray(decay_table(plan)))
    edge = pltpu.VMEM((2, plan.rows, LANES), jnp.float32)
    return pl.pallas_call(
        functools.partial(kernel, plan),
        out_shape=pltpu.VMEM(fields.shape, jnp.float32),
        in_specs=[anywhere] * 6,
        out_specs=pl.BlockSpec(memory_space=pltpu.VMEM),
        scratch_shapes=[
            *[pltpu.SMEM(table.shape, table.dtype) for table in tables],
            *[pltpu.VMEM(tables[i].shape, tables[i].dtype) for i in (0, 2, 1)],
            pltpu.VMEM((plan.rows, plan.lon), jnp.float32),
            dma((plan.fields,)),
            dma((len(tables) + 3,)),
            lines(HALO + plan.rows),
            lines(blocks * plan.slots),
            pltpu.VMEM((plan.slots, blocks, plan.cols * LANES), jnp.float32),
            pltpu.VMEM((plan.slots, 2 * LANES, 2 * LANES), jnp.bfloat16),
            lines(blocks * plan.own_a),
            lines(plan.rows),
            lines(blocks * plan.own_h),
            lines(plan.fields * HALO),
            lines(plan.fields * HALO, plan.ext),
            lines(plan.fields * HALO, plan.ext),
            lines(blocks * HALO, plan.ext),
            edge,
            edge,
            pltpu.VMEM((plan.fields * (plan.tiles + 1), 8 * (plan.cols + 1), LANES), jnp.float32),
            pltpu.VMEM((SUBS, plan.tiles, TAPS, 8, LANES), jnp.float32),
            pltpu.VMEM((SUBS, plan.tiles, 3, 8, LANES), jnp.float32),
            dma,
            dma((max(plan.groups_a, plan.groups_h),)),
            dma,
            dma,
            dma,
            dma((len(plan.south_to),)),
            dma,
            dma((n_pieces,)),
            dma,
            dma,
            dma,
            dma((2,)),
            dma((2,)),
            dma,
            dma,
            dma((plan.groups_h,)),
            dma,
            dma,
            dma((n_pieces,)),
            dma,
            dma,
            dma,
        ],
        compiler_params=pltpu.CompilerParams(
            collective_id=0, has_side_effects=True, vmem_limit_bytes=VMEM_LIMIT
        ),
        name="transport",
    )(
        *tables,
        fields.reshape(plan.rows, plan.lon),
    )


def solution(mesh):
    def whole(fields, frac_x, frac_y, shift_cells, polar_mask):
        return jax.shard_map(
            functools.partial(body, Plan(mesh, fields.shape)),
            mesh=mesh,
            in_specs=(P(None, None, "lat", "lon"), P(), P(), P(), P()),
            out_specs=P(None, None, "lat", "lon"),
            check_vma=False,
        )(fields, frac_x, frac_y, shift_cells, polar_mask)

    return whole
```

```python
import functools
import math

import jax
import jax.numpy as jnp
import numpy as np
from jax import lax
from jax.experimental import pallas as pl
from jax.experimental.pallas import tpu as pltpu
from jax.sharding import PartitionSpec as P

SUBS = 2
LANES = 128
HALO = 2
MESH = pl.DeviceIdType.MESH
HELP = (3, 10)
RELAY = (1, 3)
TAPS = 5
VMEM_LIMIT = int(58 * 1024 * 1024)


class Plan:
    def __init__(self, mesh, fields_shape):
        self.blocks = mesh.shape["lon"]
        self.bands = mesh.shape["lat"]
        self.fields, _, self.lat_total, self.lon_total = fields_shape
        self.lat = self.lat_total // self.bands
        self.lon = self.lon_total // self.blocks
        self.cols = -(-self.lon // LANES)
        self.rem = self.lon - LANES * (self.cols - 1)
        self.rows = self.fields * self.lat
        per = self.rows // self.blocks
        self.own_h = per * HELP[0] // HELP[1]
        self.own_a = per - self.own_h
        self.joint = 2 if self.own_h % 2 == 0 and self.own_a % 2 == 0 else 1
        self.unit_a = 2 * self.joint if self.own_a % (2 * self.joint) == 0 else self.joint
        self.unit_h = self.joint
        self.groups_a = self.own_a // self.unit_a
        self.groups_h = self.own_h // self.unit_h
        self.base_h = self.blocks * self.own_a
        self.relayed, self.lag = min(RELAY[0], self.groups_h), RELAY[1]
        pitch = self.cols
        while (self.joint * pitch) % 8:
            pitch += 1
        self.pitch = pitch
        self.ext = -(-(self.cols + 1) // 8) * 8
        self.slots = self.own_a + 2 * HALO
        self.tiles = self.lat // 8
        assert self.rows % self.blocks == 0 and self.own_a <= self.lat and self.bands >= 4
        assert 1 <= self.own_h <= self.own_a and self.lat % 8 == 0
        assert self.blocks & (self.blocks - 1) == 0 and self.blocks % 8 == 0
        assert HALO * SUBS + SUBS <= self.rem <= LANES - 2 * SUBS
        self.south_to = []
        for f in range(self.fields):
            for at in sorted({self.host(f * self.lat), self.host(f * self.lat + 1)}):
                self.south_to.append((f, *at))
        self.pieces = [(f, part) for f in range(self.fields) for part in range(HALO // self.joint)]

    def host(self, flat):
        if flat < self.base_h:
            return 0, flat // self.own_a
        return 1, (flat - self.base_h) // self.own_h

    def piece(self, i):
        f, part = self.pieces[i]
        flat = f * self.lat + self.lat - HALO + part * self.joint
        helper, lon = self.host(flat)
        inside = (flat - self.base_h) % self.own_h if helper else flat % self.own_a
        return helper, lon, inside


def decay_table(plan):
    rows = np.arange(plan.lat_total, dtype=np.float64)
    phi = math.pi * (rows + 0.5) / plan.lat_total - math.pi / 2
    b = np.cos(phi) / math.sin(math.pi * (plan.lat - 0.5) / plan.lat_total)
    log_r = -2.0 * np.arcsinh(b)
    r = np.exp(log_r)
    lines = [np.exp(log_r * 2**k) for k in range(7)]
    lines += [np.exp(log_r * LANES), np.exp(log_r * plan.rem)]
    lines += [(1 - r) / (1 + r), 1 / (1 - np.exp(log_r * plan.lon_total)), log_r]
    lines += [np.exp(log_r * plan.lon * 2**k) for k in range(plan.blocks.bit_length() - 1)]
    table = np.stack(lines).astype(np.float32)
    return np.where(np.abs(table) < 1.2e-38, np.float32(0), table)


def build_weights(table, row, weights, slot):
    i = lax.broadcasted_iota(jnp.int32, (LANES, LANES), 0)
    j = lax.broadcasted_iota(jnp.int32, (LANES, LANES), 1)
    apart = jnp.abs(i - j).astype(jnp.float32)
    full = table[9, row] * jnp.exp(table[11, row] * apart)
    high = full.astype(jnp.bfloat16)
    low = (full - high.astype(jnp.float32)).astype(jnp.bfloat16)
    for k in range(2):
        weights[slot, k * LANES : (k + 1) * LANES, :LANES] = high
        weights[slot, k * LANES : (k + 1) * LANES, LANES:] = low


def row_steps(plan, x, courant, count, marked, power, weights):
    blocks, cols, rem = plan.blocks, plan.cols, plan.rem
    lane = lax.broadcasted_iota(jnp.int32, (blocks, LANES), 1)
    tail = lane < rem
    x = x[:-1] + [jnp.where(tail, x[-1], 0.0)]

    half = 0.5 * (1.0 - courant)
    w0 = 1.0 - courant * (1.0 + half)
    w1 = courant * (1.0 + 2.0 * half)
    w2 = -courant * half
    west = pltpu.roll(x[-1], 1, 0)
    before1 = pltpu.roll(west, LANES + 1 - rem, 1) if rem > 1 else west
    before2 = pltpu.roll(west, LANES + 2 - rem, 1)
    zonal = []
    for c in range(cols):
        one, two = pltpu.roll(x[c], 1, 1), pltpu.roll(x[c], 2, 1)
        zonal.append(
            w0 * x[c]
            + w1 * jnp.where(lane < 1, before1, one)
            + w2 * jnp.where(lane < 2, before2, two)
        )
        before1, before2 = one, two

    count = lax.rem(count + plan.lon_total, plan.lon_total)
    moved = [pltpu.roll(z, lax.div(count, plan.lon), 0) for z in zonal]
    start = plan.lon - lax.rem(count, plan.lon)
    western = [pltpu.roll(m, 1, 0) for m in moved]
    turned = [pltpu.roll(m, rem % LANES, 1) for m in moved]
    window = western[:-1]
    for c in range(cols + 1):
        left = western[-1] if c == 0 else turned[c - 1]
        right = turned[c] if c < cols else left
        window.append(jnp.where(tail, left, right))
    first = jnp.full((blocks, LANES), start, jnp.int32) >> 7
    for k in reversed(range((cols - 1).bit_length())):
        by = 1 << k
        taken = (first & by) == by
        window = [
            jnp.where(taken, window[i + by], window[i]) if i + by < len(window) else window[i]
            for i in range(min(len(window), cols + by))
        ]
    within = start & (LANES - 1)
    window = [pltpu.roll(w, (LANES - within) & (LANES - 1), 1) for w in window]
    keep = lane < LANES - jnp.full((blocks, LANES), within, jnp.int32)
    s = [jnp.where(keep, window[c], window[c + 1]) for c in range(cols)]
    s[-1] = jnp.where(tail, s[-1], 0.0)

    r128, r_rem = power(7), power(8)
    closing, log_r = power(10), power(11)
    lane_f = lane.astype(jnp.float32)
    enter_west = jnp.exp(log_r * (lane_f + 1.0))
    enter_east = jnp.exp(log_r * (LANES - lane_f))
    enter_tail = jnp.exp(log_r * jnp.maximum(rem - lane_f, 0.0))
    stacked = jnp.concatenate(s, axis=0)
    high = stacked.astype(jnp.bfloat16)
    low = (stacked - high.astype(jnp.float32)).astype(jnp.bfloat16)
    product = jnp.dot(
        jnp.concatenate([high, low], axis=1), weights, preferred_element_type=jnp.float32
    )
    product = product[:, :LANES] + product[:, LANES:]
    y = [product[c * blocks : (c + 1) * blocks] for c in range(cols)]

    def spread(column, at):
        return jnp.broadcast_to(column[:, at : at + 1], (blocks, LANES))

    ends = [spread(y[c], LANES - 1 if c < cols - 1 else rem - 1) for c in range(cols)]
    begins = [spread(y[c], 0) for c in range(cols)]

    def closed(total, sign):
        total = pltpu.roll(total, 1 if sign > 0 else blocks - 1, 0)
        for k in range(blocks.bit_length() - 1):
            by = 1 << k
            total = total + power(12 + k) * pltpu.roll(total, by if sign > 0 else blocks - by, 0)
        return total * closing

    total = ends[0]
    for c in range(1, cols):
        total = ends[c] + (r128 if c < cols - 1 else r_rem) * total
    carry = closed(total, 1)
    for c in range(cols):
        y[c] = y[c] + enter_west * carry
        carry = ends[c] + r128 * carry
    total = begins[-1]
    for c in range(cols - 2, -1, -1):
        total = begins[c] + r128 * total
    carry = closed(total, -1)
    for c in range(cols - 1, -1, -1):
        y[c] = y[c] + (enter_tail if c == cols - 1 else enter_east) * carry
        carry = begins[c] + (r_rem if c == cols - 1 else r128) * carry
    filtered = jnp.full((blocks, LANES), marked, jnp.int32) == 1
    return [jnp.where(filtered, y[c], s[c]) for c in range(cols)]


def face_weights(plan, cy, t, row):
    last = plan.lat_total - 1
    c0 = jnp.where(row == 0, 0.0, cy[t, 0, row])
    c1 = jnp.where(row == last, 0.0, cy[t, 0, jnp.minimum(row + 1, last)])
    h0, h1 = 0.5 * (1.0 - c0), 0.5 * (1.0 - c1)
    return 1.0 - c1 * (1.0 + h1), c1 * h1 + c0 * (1.0 + h0), -c0 * h0


def start_all(copies):
    for copy in copies:
        copy.start()


def west_edge(plan, tail):
    return pltpu.roll(tail, LANES - plan.rem, tail.ndim - 1)


def east_edge(plan, first):
    return pltpu.roll(first, plan.rem, first.ndim - 1)


def zonal_taps(tiles, coef, lane, wanted):
    count = len(tiles)
    ahead = {}
    for c in range(max(min(wanted) - 1, 0), max(wanted) + 1):
        x = pltpu.roll(tiles[c], LANES - 2, 1)
        if c + 1 < count:
            x = jnp.where(lane >= LANES - 2, pltpu.roll(tiles[c + 1], LANES - 2, 1), x)
        u = jnp.where(coef[4] > 0.5, x, tiles[c])
        ahead[c] = [u] + [pltpu.roll(u, k, 1) for k in range(1, 4)]
    out = []
    for c in wanted:
        total = coef[0] * ahead[c][0]
        for k in range(1, 4):
            x = ahead[c][k]
            if c > 0:
                x = jnp.where(lane < k, ahead[c - 1][k], x)
            total = total + coef[k] * x
        out.append(total)
    return out


def kernel(plan, *refs):
    inputs, (x_ref, out_ref), tables, rest = refs[:5], refs[5:7], refs[7:15], refs[15:]
    cx, cy, shift, mask, table, cxv, shv, cyv = tables
    (x_local, x_sem, table_sem, packed, arrived, held, weights, ready, got, stage, got_south,
    f1_south, f1_out, ext, edge_out, edge_in, f1, taps, merid,
    in_send, in_recv, halo_send, halo_recv, own_in,
    south_in_send, south_in_recv, ext_send, ext_recv, f1_send, f1_recv, edge_send, edge_recv,
    out_send, out_recv, stage_recv, back_send, back_recv,
    south_out_send, south_out_recv, f2_send, f2_recv) = rest
    blocks, pitch, cols, lat, rem = plan.blocks, plan.pitch, plan.cols, plan.lat, plan.rem
    slots, bands, tiles, joint = plan.slots, plan.bands, plan.tiles, plan.joint
    unit_of = (plan.unit_a, plan.unit_h)
    me = lax.axis_index("lon")
    band = lax.axis_index("lat")
    low = band < 2
    polar = jnp.logical_or(band == 0, band == bands - 1)
    mid = jnp.logical_not(polar)
    helper = jnp.logical_or(band == 1, band == bands - 2)
    worker = jnp.logical_or(polar, helper)
    pole = jnp.where(low, 0, bands - 1)
    help_band = jnp.where(low, 1, bands - 2)
    mate = jnp.where(polar, help_band, pole)
    north_mid = jnp.logical_and(band >= 1, band < bands - 2)
    south_mid = jnp.logical_and(band >= 2, band < bands - 1)
    own = jnp.where(helper, plan.own_h, plan.own_a)
    count = jnp.where(helper, plan.groups_h, plan.groups_a)
    unit = jnp.where(helper, plan.unit_h, plan.unit_a)
    base = jnp.where(helper, plan.base_h, 0)

    def peer(k):
        return lax.rem(me + k, blocks)

    def at(lon, lat_at):
        return {"lon": lon, "lat": lat_at}

    barrier = pltpu.get_barrier_semaphore()

    def greet(lon, lat_at):
        pl.semaphore_signal(barrier, inc=1, device_id=at(lon, lat_at), device_id_type=MESH)

    @pl.when(worker)
    def _():
        for k in range(blocks):
            greet(peer(k), mate)
        for k in range(1, blocks):
            greet(peer(k), band)

    @pl.when(jnp.logical_not(worker))
    def _():
        greet(peer(1), band)
        greet(peer(blocks - 1), band)

    @pl.when(south_mid)
    def _():
        greet(me, band - 1)

    def lines(first, rows, wide=pitch):
        return pl.ds(pl.multiple_of(first * wide, 8), rows * wide)

    def load(f):
        part = pl.ds(f * lat, lat)
        return pltpu.make_async_copy(x_ref.at[part], x_local.at[part], x_sem.at[f])

    start_all([load(f) for f in range(plan.fields)])
    sources = inputs[:5] + (inputs[0], inputs[2], inputs[1])
    table_copies = [
        pltpu.make_async_copy(source, to, table_sem.at[i])
        for i, (source, to) in enumerate(zip(sources, tables))
    ]
    start_all(table_copies)
    packed[0 : HALO * pitch, :] = jnp.zeros((HALO * pitch, LANES), jnp.float32)
    lane = lax.broadcasted_iota(jnp.int32, (8, LANES), 1)
    sub = lax.broadcasted_iota(jnp.int32, (8, LANES), 0)

    def tile_of(part, c):
        width = LANES if c < cols - 1 else rem
        v = x_local[pl.ds(pl.multiple_of(part * 8, 8), 8), c * LANES : c * LANES + width]
        if width < LANES:
            v = jnp.concatenate([v, jnp.zeros((8, LANES - width), jnp.float32)], axis=1)
        return v

    def fill(part, none):
        for c in range(cols):
            packed[pl.ds((part * 8 + HALO) * pitch + c, 8, stride=pitch), :] = tile_of(part, c)
        return none

    def edges(part, none):
        rows = pl.ds(pl.multiple_of(part * 8, 8), 8)
        edge_out[0, rows, :] = west_edge(plan, tile_of(part, cols - 1))
        edge_out[1, rows, :] = east_edge(plan, tile_of(part, 0))
        return none

    for copy in table_copies:
        copy.wait()
    for f in range(plan.fields):
        load(f).wait()

    @pl.when(polar)
    def _():
        lax.fori_loop(0, plan.rows // 8, fill, 0)

    @pl.when(mid)
    def _():
        lax.fori_loop(0, plan.rows // 8, edges, 0, unroll=5)
        lax.fori_loop(0, plan.fields, lambda f, none: fill(f * tiles + tiles - 1, none), 0)

    row_id = lax.broadcasted_iota(jnp.int32, (8, plan.lat_total), 1)
    row_sub = lax.broadcasted_iota(jnp.int32, (8, plan.lat_total), 0)

    def rows_of(vector, first):
        hit = row_id == row_sub + first
        one = jnp.sum(jnp.where(hit, vector, 0.0), axis=1, keepdims=True)
        return jnp.broadcast_to(one, (8, LANES))

    for t in range(SUBS):
        for g in range(tiles):
            first = band * lat + g * 8
            c0 = jnp.where(sub + first == 0, 0.0, rows_of(cyv[t], first))
            c1 = rows_of(cyv[t], first + 1)
            h0, h1 = 0.5 * (1.0 - c0), 0.5 * (1.0 - c1)
            merid[t, g, 0] = 1.0 - c1 * (1.0 + h1)
            merid[t, g, 1] = c1 * h1 + c0 * (1.0 + h0)
            merid[t, g, 2] = -c0 * h0

    @pl.when(mid)
    def _():
        for t in range(SUBS):
            for g in range(tiles):
                first = band * lat + g * 8
                courant = rows_of(cxv[t], first)
                moved = rows_of(shv[t].astype(jnp.float32), first)
                half = 0.5 * (1.0 - courant)
                w0 = 1.0 - courant * (1.0 + half)
                w1 = courant * (1.0 + 2.0 * half)
                w2 = -courant * half
                ahead = moved < -0.5
                still = moved == jnp.where(ahead, -2.0, 0.0)
                taps[t, g, 0] = jnp.where(still, w0, 0.0)
                taps[t, g, 1] = jnp.where(still, w1, w0)
                taps[t, g, 2] = jnp.where(still, w2, w1)
                taps[t, g, 3] = jnp.where(still, 0.0, w2)
                taps[t, g, 4] = jnp.where(ahead, 1.0, 0.0)

    def place(slot):
        flat = base + me * own + slot - HALO
        south = slot >= slots - HALO
        row = jnp.where(south, slot - slots, lax.rem(flat + lat, lat))
        return south, jnp.maximum(pole * lat + row, 0)

    def build(i, none):
        for n in (2 * i, 2 * i + 1) if plan.joint == 2 else (i,):
            slot = jnp.where(n < own + HALO, n, n + slots - 2 * HALO - own)
            build_weights(table, place(slot)[1], weights, slot)
        return none

    @pl.when(polar)
    def _():
        lax.fori_loop(0, (own + 2 * HALO) // plan.joint, build, 0)

    def taps_of(t, i):
        g = lax.rem(i, tiles)
        return [taps[t, g, n] for n in range(TAPS)]

    def put(i, c, v):
        f1[i + i // tiles + 1, c * 8 : c * 8 + 8, :] = v

    def stepped(i, wanted):
        f, g = i // tiles, lax.rem(i, tiles)
        a = [merid[0, g, n] for n in range(3)]
        out = []
        for c in wanted:
            old = f1[i + f, c * 8 : c * 8 + 8, :]
            now = f1[i + f + 1, c * 8 : c * 8 + 8, :]
            one = jnp.where(sub < 1, pltpu.roll(old, 1, 0), pltpu.roll(now, 1, 0))
            two = jnp.where(sub < 2, pltpu.roll(old, 2, 0), pltpu.roll(now, 2, 0))
            out.append(a[0] * now + a[1] * one + a[2] * two)
        return out

    def keep(i, c, v):
        got[pl.ds(i * 8 * pitch + c, 8, stride=pitch), :] = v

    def first_inside(i, none):
        x = [tile_of(i, c) for c in range(cols)]
        for c, v in enumerate(zonal_taps(x, taps_of(0, i), lane, range(cols))):
            put(i, c + 1, v)
        return none

    def second_inside(i, none):
        x = stepped(i, range(1, cols + 1))
        inner = range(1, cols - 1)
        for c, v in zip(inner, zonal_taps(x, taps_of(1, i), lane, inner)):
            keep(i, c, v)
        return none

    def first_edges(i, none):
        rows = pl.ds(pl.multiple_of(i * 8, 8), 8)
        coef = taps_of(0, i)
        x = [edge_in[0, rows, :], tile_of(i, 0), tile_of(i, 1)]
        for c, v in enumerate(zonal_taps(x, coef, lane, range(2))):
            put(i, c, v)
        x = [tile_of(i, cols - 2), tile_of(i, cols - 1)]
        x[1] = jnp.where(lane < rem, x[1], edge_in[1, rows, :])
        put(i, cols, zonal_taps(x, coef, lane, [1])[0])
        return none

    def second_edges(i, none):
        coef = taps_of(1, i)
        keep(i, 0, zonal_taps(stepped(i, range(3)), coef, lane, [1])[0])
        keep(i, cols - 1, zonal_taps(stepped(i, [cols - 1, cols]), coef, lane, [1])[0])
        return none

    def northern(each, unroll):
        def at_tile(i, none):
            return each(i // (tiles - 1) * tiles + lax.rem(i, tiles - 1) + 1, none)

        lax.fori_loop(0, plan.fields * (tiles - 1), at_tile, 0, unroll=unroll)

    @pl.when(mid)
    def _():
        lax.fori_loop(0, plan.rows // 8, first_inside, 0, unroll=2)
        northern(second_inside, 3)

    pl.semaphore_wait(
        barrier,
        jnp.where(worker, 2 * blocks - 1, 2) + jnp.where(north_mid, 1, 0),
    )

    def remote(src, dst, send, recv, lon, lat_at):
        return pltpu.make_async_remote_copy(
            src_ref=src,
            dst_ref=dst,
            send_sem=send,
            recv_sem=recv,
            device_id=at(lon, lat_at),
            device_id_type=MESH,
        )

    def taken(ref, rows, sem, wide=pitch):
        part = ref.at[pl.ds(0, rows * wide)]
        pltpu.make_async_copy(part, part, sem).wait()

    def rows_in(role, k, g):
        own_r, first = (plan.own_h, plan.base_h) if role else (plan.own_a, 0)
        to = peer(k)
        step_rows = unit_of[role]
        return remote(
            packed.at[lines(HALO + first + to * own_r + g * step_rows, step_rows)],
            arrived.at[lines(me * slots + HALO + g * step_rows, step_rows)],
            in_send,
            in_recv.at[g],
            to,
            help_band if role else band,
        )

    def halo_in(role, k):
        own_r, first = (plan.own_h, plan.base_h) if role else (plan.own_a, 0)
        to = peer(k)
        return remote(
            packed.at[lines(first + to * own_r, HALO)],
            arrived.at[lines(me * slots, HALO)],
            halo_send,
            halo_recv,
            to,
            help_band if role else band,
        )

    own_copy = pltpu.make_async_copy(
        packed.at[lines(me * plan.own_a, plan.own_a + HALO)],
        arrived.at[lines(me * slots, plan.own_a + HALO)],
        own_in,
    )

    def start_in():
        for k in range(1, blocks):
            halo_in(0, k).start()
        for k in range(blocks):
            halo_in(1, k).start()
        for g in range(max(plan.groups_a, plan.groups_h)):
            for role in (1, 0):
                if g < (plan.groups_h if role else plan.groups_a):
                    for k in range(0 if role else 1, blocks):
                        rows_in(role, k, g).start()

    @pl.when(polar)
    def _():
        own_copy.start()
        start_in()

    def edge_copy(i):
        to = peer(1 if i == 0 else blocks - 1)
        return remote(edge_out.at[i], edge_in.at[i], edge_send.at[i], edge_recv.at[i], to, band)

    def south_parts(i):
        f, role, d = plan.south_to[i]
        src = packed.at[lines(HALO + f * lat + lat - HALO, HALO)]
        dst = arrived.at[lines(me * slots + slots - HALO, HALO)]
        return role, d, src, dst

    def south_in(i):
        role, d, src, dst = south_parts(i)
        return remote(
            src,
            dst,
            south_in_send.at[i],
            south_in_recv,
            jnp.int32(d),
            jnp.int32(bands - 2 if role else bands - 1),
        )

    def each_south_in(act, local):
        for i in range(len(plan.south_to)):
            role, d, src, dst = south_parts(i)
            if role:

                @pl.when(me != d)
                def _():
                    act(south_in(i))

                @pl.when(me == d)
                def _():
                    if local:
                        pltpu.make_async_copy(src, dst, south_in_recv).start()

            else:
                act(south_in(i))

    @pl.when(mid)
    def _():
        start_all([edge_copy(0), edge_copy(1)])

    @pl.when(band == bands - 2)
    def _():
        each_south_in(lambda copy: copy.start(), True)

    def show_north(f, none):
        for c in range(cols + 1):
            f1_out[pl.ds(f * HALO * plan.ext + c, HALO, stride=plan.ext), :] = f1[
                (f + 1) * (tiles + 1) - 1, c * 8 + 8 - HALO : c * 8 + 8, :
            ]
        return none

    f1_copy = remote(f1_out, f1_south, f1_send, f1_recv, me, band + 1)

    def f2_copy(f):
        return remote(
            got.at[lines(f * lat + lat - HALO, HALO)],
            got_south.at[lines(f * HALO, HALO)],
            f2_send,
            f2_recv,
            me,
            band + 1,
        )

    @pl.when(helper)
    def _():
        lax.fori_loop(0, (own + 2 * HALO) // plan.joint, build, 0)

    def close_first():
        for i in range(2):
            edge_copy(i).wait_recv()
        lax.fori_loop(0, plan.rows // 8, first_edges, 0, unroll=5)

        @pl.when(north_mid)
        def _():
            lax.fori_loop(0, plan.fields, show_north, 0, unroll=True)
            f1_copy.start()

    def close_second():
        northern(second_edges, 5)
        start_all([f2_copy(f) for f in range(plan.fields)])

    def steps(x, t, row, slot):
        return row_steps(
            plan,
            x,
            cx[t, 0, row],
            shift[t, 0, row],
            mask[row],
            lambda i: table[i, row],
            weights[slot],
        )

    def first_pass(slot):
        _, row = place(slot)
        x = [arrived[pl.ds(slot * pitch + c, blocks, stride=slots * pitch), :] for c in range(cols)]
        y = steps(x, 0, row, slot)
        for c in range(cols):
            held[slot, :, c * LANES : (c + 1) * LANES] = y[c]

    def second_pass(m):
        j = lax.rem(base + me * own + m, lat)
        row = pole * lat + j
        s0 = m + HALO
        s1 = jnp.where(j == 0, slots - 1, s0 - 1)
        s2 = jnp.where(j == 0, slots - 2, jnp.where(j == 1, slots - 1, s0 - 2))
        a0, a1, a2 = face_weights(plan, cy, 0, row)
        x = []
        for c in range(cols):
            part = slice(c * LANES, (c + 1) * LANES)
            x.append(a0 * held[s0, :, part] + a1 * held[s1, :, part] + a2 * held[s2, :, part])
        y = steps(x, 1, row, s0)
        for c in range(cols):
            ready[pl.ds(m * pitch + c, blocks, stride=plan.own_a * pitch), :] = y[c]

    def hosts(i):
        role, lon, _ = plan.piece(i)
        return jnp.logical_and(me == lon, band == role)

    def ext_parts(i, k):
        f, part = plan.pieces[i]
        src = ext.at[lines((part * blocks + peer(k)) * joint, joint, plan.ext)]
        return src, f1_south.at[lines(f * HALO + part * joint, joint, plan.ext)]

    def f2_parts(i, k):
        f, part = plan.pieces[i]
        src = ready.at[lines(peer(k) * plan.own_a + plan.piece(i)[2], joint)]
        return src, got_south.at[lines(f * HALO + part * joint, joint)]

    def piece_copies(i, parts, send, recv):
        helps = plan.piece(i)[0]
        return [
            remote(*parts(i, k), send.at[i], recv, peer(k), jnp.int32(1))
            for k in range(1 if helps else 0, blocks)
        ]

    def piece_start(i, parts, send, recv):
        start_all(piece_copies(i, parts, send, recv))
        if plan.piece(i)[0]:
            pltpu.make_async_copy(*parts(i, 0), recv).start()

    wide_lane = lax.broadcasted_iota(jnp.int32, (blocks, LANES), 1)

    def widen(i):
        _, _, inside = plan.piece(i)
        part = plan.pieces[i][1]
        for u in range(joint):
            x = [held[inside + u + HALO, :, c * LANES : (c + 1) * LANES] for c in range(cols)]
            west = west_edge(plan, pltpu.roll(x[-1], 1, 0))
            east = east_edge(plan, pltpu.roll(x[0], blocks - 1, 0))
            x[-1] = jnp.where(wide_lane < rem, x[-1], east)
            for c, v in enumerate([west] + x):
                first = (part * blocks * joint + u) * plan.ext + c
                ext[pl.ds(first, blocks, stride=joint * plan.ext), :] = v

    def each_row(g, do):
        def some(i, none):
            for u in range(joint):
                do(g * unit + i * joint + u)
            return none

        lax.fori_loop(0, unit // joint, some, 0)

    def first_group(g):
        @pl.when(polar)
        def _():
            taken(arrived, (blocks - 1) * plan.unit_a, in_recv.at[g])

        @pl.when(helper)
        def _():
            taken(arrived, blocks * plan.unit_h, in_recv.at[g])

        each_row(g, lambda m: first_pass(m + HALO))
        for i in range(len(plan.pieces)):

            @pl.when(jnp.logical_and(hosts(i), g == plan.piece(i)[2] // unit_of[plan.piece(i)[0]]))
            def _():
                widen(i)
                piece_start(i, ext_parts, ext_send, ext_recv)

    is_host = False
    for _, role, d in plan.south_to:
        its = bands - 2 if role else bands - 1
        is_host = jnp.logical_or(is_host, jnp.logical_and(me == d, band == its))

    def others():
        @pl.when(polar)
        def _():
            taken(arrived, (blocks - 1) * HALO, halo_recv)

        @pl.when(helper)
        def _():
            taken(arrived, blocks * HALO, halo_recv)

        @pl.when(is_host)
        def _():
            taken(arrived, blocks * HALO, south_in_recv)

        def two(i, none):
            for u in range(HALO):
                first_pass(i * (slots - HALO) + u)
            return none

        lax.fori_loop(0, 1 + jnp.where(is_host, 1, 0), two, 0)

    def own_back(g):
        rows = plan.unit_a
        part = pl.multiple_of((me * plan.own_a + g * rows) * pitch, 8)
        part = pl.ds(part, rows * pitch)
        return pltpu.make_async_copy(ready.at[part], got.at[part], out_recv)

    def own_stage(g):
        rows = plan.unit_h
        return pltpu.make_async_copy(
            ready.at[lines(me * plan.own_a + g * rows, rows)],
            stage.at[lines(me * plan.own_h + g * rows, rows)],
            stage_recv.at[g],
        )

    def rows_out(k, g):
        rows = plan.unit_a
        return remote(
            ready.at[lines(peer(k) * plan.own_a + g * rows, rows)],
            got.at[lines(me * plan.own_a + g * rows, rows)],
            out_send,
            out_recv,
            peer(k),
            band,
        )

    def rows_home(k, g):
        rows = plan.unit_h
        return remote(
            ready.at[lines(peer(k) * plan.own_a + g * rows, rows)],
            got.at[lines(plan.base_h + me * plan.own_h + g * rows, rows)],
            out_send,
            back_recv,
            peer(k),
            mate,
        )

    def rows_stage(k, g):
        rows = plan.unit_h
        return remote(
            ready.at[lines(peer(k) * plan.own_a + g * rows, rows)],
            stage.at[lines(me * plan.own_h + g * rows, rows)],
            out_send,
            stage_recv.at[g],
            peer(k),
            band,
        )

    def relay(g):
        taken(stage, blocks * plan.unit_h, stage_recv.at[g])
        wide = plan.own_h * pitch
        part = pl.ds(pl.multiple_of(g * plan.unit_h * pitch, 8), plan.unit_h * pitch)
        landing = got.at[pl.ds(plan.base_h * pitch, blocks * wide)]
        remote(
            stage.reshape(blocks, wide, LANES).at[:, part, :],
            landing.reshape(blocks, wide, LANES).at[:, part, :],
            back_send,
            back_recv,
            me,
            mate,
        ).start()

    def ship(g):
        @pl.when(polar)
        def _():
            start_all([rows_out(k, g) for k in range(1, blocks)])
            own_back(g).start()

        @pl.when(helper)
        def _():
            @pl.when(g < plan.relayed)
            def _():
                start_all([rows_stage(k, g) for k in range(1, blocks)])
                own_stage(g).start()

            @pl.when(g >= plan.relayed)
            def _():
                start_all([rows_home(k, g) for k in range(blocks)])

        for i in range(len(plan.pieces)):

            @pl.when(jnp.logical_and(hosts(i), g == plan.piece(i)[2] // unit_of[plan.piece(i)[0]]))
            def _():
                piece_start(i, f2_parts, south_out_send, south_out_recv)

    @pl.when(polar)
    def _():
        own_copy.wait()

    @pl.when(jnp.logical_and(worker, low))
    def _():
        held[slots - HALO :, :, :] = jnp.zeros((HALO, blocks, cols * LANES), jnp.float32)

    def step(s, none):
        first_group(s)
        each_row(s, second_pass)
        ship(s)

        @pl.when(jnp.logical_and(helper, s == 0))
        def _():
            close_first()

        @pl.when(jnp.logical_and(helper, s == min(1, plan.groups_h - 1)))
        def _():
            close_second()

        @pl.when(jnp.logical_and(helper, jnp.logical_and(s >= plan.lag, s < plan.relayed + plan.lag)))
        def _():
            relay(s - plan.lag)

        return none

    if bands > 4:

        @pl.when(jnp.logical_not(worker))
        def _():
            close_first()
            close_second()

    @pl.when(worker)
    def _():
        others()
        lax.fori_loop(0, count, step, 0)

        @pl.when(helper)
        def _():
            for g in range(max(plan.groups_h - plan.lag, 0), plan.relayed):
                relay(g)

    @pl.when(band == 1)
    def _():
        taken(f1_south, plan.fields * HALO, ext_recv, plan.ext)

    @pl.when(south_mid)
    def _():
        remote(f1_out, f1_south, f1_send, f1_recv, me, band + 1).wait_recv()

    @pl.when(mid)
    def _():
        def outer(f, none):
            for c in range(cols + 1):
                f1[f * (tiles + 1), c * 8 + 8 - HALO : c * 8 + 8, :] = f1_south[
                    pl.ds(f * HALO * plan.ext + c, HALO, stride=plan.ext), :
                ]
            i = f * tiles
            x = stepped(i, range(cols + 1))
            for c, v in enumerate(zonal_taps(x, taps_of(1, i), lane, range(1, cols + 1))):
                keep(i, c, v)
            return none

        lax.fori_loop(0, plan.fields, outer, 0)

    @pl.when(polar)
    def _():
        taken(got, plan.base_h, out_recv)

    @pl.when(band == 0)
    def _():
        got_south[...] = jnp.zeros_like(got_south)

    @pl.when(band == 1)
    def _():
        taken(got_south, plan.fields * HALO, south_out_recv)

    @pl.when(band >= 2)
    def _():
        taken(got_south, plan.fields * HALO, f2_recv)

    def one_field(f, none):
        for g in range(tiles):
            a0, a1, a2 = (merid[SUBS - 1, g, i] for i in range(3))
            for c in range(cols):
                first = (f * lat + g * 8) * pitch + c
                x0 = got[pl.ds(first, 8, stride=pitch), :]
                if g:
                    x1 = got[pl.ds(first - pitch, 8, stride=pitch), :]
                    x2 = got[pl.ds(first - 2 * pitch, 8, stride=pitch), :]
                else:
                    south2 = got_south[pl.ds(f * HALO * pitch + c, 1), :]
                    south1 = got_south[pl.ds((f * HALO + 1) * pitch + c, 1), :]
                    x1 = jnp.where(sub == 0, south1, pltpu.roll(x0, 1, 0))
                    x2 = jnp.where(
                        sub == 0, south2, jnp.where(sub == 1, south1, pltpu.roll(x0, 2, 0))
                    )
                v = a0 * x0 + a1 * x1 + a2 * x2
                width = LANES if c < cols - 1 else rem
                out_ref[f, 0, g * 8 : g * 8 + 8, c * LANES : c * LANES + width] = v[:, :width]
        return none

    early = plan.base_h // lat
    lax.fori_loop(0, early, one_field, 0)

    @pl.when(polar)
    def _():
        taken(got, plan.rows - plan.base_h, back_recv)

    lax.fori_loop(early, plan.fields, one_field, 0)

    @pl.when(polar)
    def _():
        taken(packed, (blocks - 1) * plan.own_a + blocks * plan.own_h, in_send)
        taken(ready, (blocks - 1) * plan.own_a, out_send)

        taken(packed, (2 * blocks - 1) * HALO, halo_send)

    @pl.when(helper)
    def _():
        straight = plan.own_h - plan.relayed * plan.unit_h
        taken(ready, (blocks - 1) * plan.own_h + straight, out_send)
        if plan.relayed:
            taken(stage, blocks * plan.relayed * plan.unit_h, back_send)

    for i in range(len(plan.pieces)):

        @pl.when(hosts(i))
        def _():
            sent = blocks - plan.piece(i)[0]
            taken(ext, sent * joint, ext_send.at[i], plan.ext)
            taken(ready, sent * joint, south_out_send.at[i])

    @pl.when(band == bands - 2)
    def _():
        each_south_in(lambda copy: copy.wait_send(), False)

    @pl.when(north_mid)
    def _():
        f1_copy.wait_send()

    @pl.when(mid)
    def _():
        for i in range(2):
            edge_copy(i).wait_send()
        taken(got, plan.fields * HALO, f2_send)


def body(plan, fields, frac_x, frac_y, shift_cells, polar_mask):
    blocks, pitch = plan.blocks, plan.pitch
    anywhere = pl.BlockSpec(memory_space=pltpu.HBM)
    dma = pltpu.SemaphoreType.DMA
    n_pieces = len(plan.pieces)

    def lines(rows, wide=pitch):
        return pltpu.VMEM((rows * wide, LANES), jnp.float32)

    tables = (frac_x, frac_y, shift_cells, polar_mask, jnp.asarray(decay_table(plan)))
    edge = pltpu.VMEM((2, plan.rows, LANES), jnp.float32)
    return pl.pallas_call(
        functools.partial(kernel, plan),
        out_shape=pltpu.VMEM(fields.shape, jnp.float32),
        in_specs=[anywhere] * 6,
        out_specs=pl.BlockSpec(memory_space=pltpu.VMEM),
        scratch_shapes=[
            *[pltpu.SMEM(table.shape, table.dtype) for table in tables],
            *[pltpu.VMEM(tables[i].shape, tables[i].dtype) for i in (0, 2, 1)],
            pltpu.VMEM((plan.rows, plan.lon), jnp.float32),
            dma((plan.fields,)),
            dma((len(tables) + 3,)),
            lines(HALO + plan.rows),
            lines(blocks * plan.slots),
            pltpu.VMEM((plan.slots, blocks, plan.cols * LANES), jnp.float32),
            pltpu.VMEM((plan.slots, 2 * LANES, 2 * LANES), jnp.bfloat16),
            lines(blocks * plan.own_a),
            lines(plan.rows),
            lines(blocks * plan.own_h),
            lines(plan.fields * HALO),
            lines(plan.fields * HALO, plan.ext),
            lines(plan.fields * HALO, plan.ext),
            lines(blocks * HALO, plan.ext),
            edge,
            edge,
            pltpu.VMEM((plan.fields * (plan.tiles + 1), 8 * (plan.cols + 1), LANES), jnp.float32),
            pltpu.VMEM((SUBS, plan.tiles, TAPS, 8, LANES), jnp.float32),
            pltpu.VMEM((SUBS, plan.tiles, 3, 8, LANES), jnp.float32),
            dma,
            dma((max(plan.groups_a, plan.groups_h),)),
            dma,
            dma,
            dma,
            dma((len(plan.south_to),)),
            dma,
            dma((n_pieces,)),
            dma,
            dma,
            dma,
            dma((2,)),
            dma((2,)),
            dma,
            dma,
            dma((plan.groups_h,)),
            dma,
            dma,
            dma((n_pieces,)),
            dma,
            dma,
            dma,
        ],
        compiler_params=pltpu.CompilerParams(
            collective_id=0, has_side_effects=True, vmem_limit_bytes=VMEM_LIMIT
        ),
        name="transport",
    )(
        *tables,
        fields.reshape(plan.rows, plan.lon),
    )


def solution(mesh):
    def whole(fields, frac_x, frac_y, shift_cells, polar_mask):
        return jax.shard_map(
            functools.partial(body, Plan(mesh, fields.shape)),
            mesh=mesh,
            in_specs=(P(None, None, "lat", "lon"), P(), P(), P(), P()),
            out_specs=P(None, None, "lat", "lon"),
            check_vma=False,
        )(fields, frac_x, frac_y, shift_cells, polar_mask)

    return whole
```

```python
import functools
import math

import jax
import jax.numpy as jnp
import numpy as np
from jax import lax
from jax.experimental import pallas as pl
from jax.experimental.pallas import tpu as pltpu
from jax.sharding import PartitionSpec as P

SUBS = 2
LANES = 128
HALO = 2
MESH = pl.DeviceIdType.MESH
HELP = (3, 10)
RELAY = (1, 3)
TAPS = 5
VMEM_LIMIT = int(58 * 1024 * 1024)


class Plan:
    def __init__(self, mesh, fields_shape):
        self.blocks = mesh.shape["lon"]
        self.bands = mesh.shape["lat"]
        self.fields, _, self.lat_total, self.lon_total = fields_shape
        self.lat = self.lat_total // self.bands
        self.lon = self.lon_total // self.blocks
        self.cols = -(-self.lon // LANES)
        self.rem = self.lon - LANES * (self.cols - 1)
        self.rows = self.fields * self.lat
        per = self.rows // self.blocks
        self.own_h = per * HELP[0] // HELP[1]
        self.own_a = per - self.own_h
        self.joint = 2 if self.own_h % 2 == 0 and self.own_a % 2 == 0 else 1
        self.unit_a = 2 * self.joint if self.own_a % (2 * self.joint) == 0 else self.joint
        self.unit_h = self.joint
        self.groups_a = self.own_a // self.unit_a
        self.groups_h = self.own_h // self.unit_h
        self.base_h = self.blocks * self.own_a
        self.relayed, self.lag = min(RELAY[0], self.groups_h), RELAY[1]
        pitch = self.cols
        while (self.joint * pitch) % 8:
            pitch += 1
        self.pitch = pitch
        self.ext = -(-(self.cols + 1) // 8) * 8
        self.slots = self.own_a + 2 * HALO
        self.tiles = self.lat // 8
        assert self.rows % self.blocks == 0 and self.own_a <= self.lat and self.bands >= 4
        assert 1 <= self.own_h <= self.own_a and self.lat % 8 == 0
        assert self.blocks & (self.blocks - 1) == 0 and self.blocks % 8 == 0
        assert HALO * SUBS + SUBS <= self.rem <= LANES - 2 * SUBS
        self.south_to = []
        for f in range(self.fields):
            for at in sorted({self.host(f * self.lat), self.host(f * self.lat + 1)}):
                self.south_to.append((f, *at))
        self.pieces = [(f, part) for f in range(self.fields) for part in range(HALO // self.joint)]

    def host(self, flat):
        if flat < self.base_h:
            return 0, flat // self.own_a
        return 1, (flat - self.base_h) // self.own_h

    def piece(self, i):
        f, part = self.pieces[i]
        flat = f * self.lat + self.lat - HALO + part * self.joint
        helper, lon = self.host(flat)
        inside = (flat - self.base_h) % self.own_h if helper else flat % self.own_a
        return helper, lon, inside


def decay_table(plan):
    rows = np.arange(plan.lat_total, dtype=np.float64)
    phi = math.pi * (rows + 0.5) / plan.lat_total - math.pi / 2
    b = np.cos(phi) / math.sin(math.pi * (plan.lat - 0.5) / plan.lat_total)
    log_r = -2.0 * np.arcsinh(b)
    r = np.exp(log_r)
    lines = [np.exp(log_r * 2**k) for k in range(7)]
    lines += [np.exp(log_r * LANES), np.exp(log_r * plan.rem)]
    lines += [(1 - r) / (1 + r), 1 / (1 - np.exp(log_r * plan.lon_total)), log_r]
    lines += [np.exp(log_r * plan.lon * 2**k) for k in range(plan.blocks.bit_length() - 1)]
    table = np.stack(lines).astype(np.float32)
    return np.where(np.abs(table) < 1.2e-38, np.float32(0), table)


def build_weights(table, row, weights, slot):
    i = lax.broadcasted_iota(jnp.int32, (LANES, LANES), 0)
    j = lax.broadcasted_iota(jnp.int32, (LANES, LANES), 1)
    apart = jnp.abs(i - j).astype(jnp.float32)
    full = table[9, row] * jnp.exp(table[11, row] * apart)
    high = full.astype(jnp.bfloat16)
    low = (full - high.astype(jnp.float32)).astype(jnp.bfloat16)
    for k in range(2):
        weights[slot, k * LANES : (k + 1) * LANES, :LANES] = high
        weights[slot, k * LANES : (k + 1) * LANES, LANES:] = low


def row_steps(plan, x, courant, count, marked, power, weights):
    blocks, cols, rem = plan.blocks, plan.cols, plan.rem
    lane = lax.broadcasted_iota(jnp.int32, (blocks, LANES), 1)
    tail = lane < rem
    x = x[:-1] + [jnp.where(tail, x[-1], 0.0)]

    half = 0.5 * (1.0 - courant)
    w0 = 1.0 - courant * (1.0 + half)
    w1 = courant * (1.0 + 2.0 * half)
    w2 = -courant * half
    west = pltpu.roll(x[-1], 1, 0)
    before1 = pltpu.roll(west, LANES + 1 - rem, 1) if rem > 1 else west
    before2 = pltpu.roll(west, LANES + 2 - rem, 1)
    zonal = []
    for c in range(cols):
        one, two = pltpu.roll(x[c], 1, 1), pltpu.roll(x[c], 2, 1)
        zonal.append(
            w0 * x[c]
            + w1 * jnp.where(lane < 1, before1, one)
            + w2 * jnp.where(lane < 2, before2, two)
        )
        before1, before2 = one, two

    count = lax.rem(count + plan.lon_total, plan.lon_total)
    moved = [pltpu.roll(z, lax.div(count, plan.lon), 0) for z in zonal]
    start = plan.lon - lax.rem(count, plan.lon)
    western = [pltpu.roll(m, 1, 0) for m in moved]
    turned = [pltpu.roll(m, rem % LANES, 1) for m in moved]
    window = western[:-1]
    for c in range(cols + 1):
        left = western[-1] if c == 0 else turned[c - 1]
        right = turned[c] if c < cols else left
        window.append(jnp.where(tail, left, right))
    first = jnp.full((blocks, LANES), start, jnp.int32) >> 7
    for k in reversed(range((cols - 1).bit_length())):
        by = 1 << k
        taken = (first & by) == by
        window = [
            jnp.where(taken, window[i + by], window[i]) if i + by < len(window) else window[i]
            for i in range(min(len(window), cols + by))
        ]
    within = start & (LANES - 1)
    window = [pltpu.roll(w, (LANES - within) & (LANES - 1), 1) for w in window]
    keep = lane < LANES - jnp.full((blocks, LANES), within, jnp.int32)
    s = [jnp.where(keep, window[c], window[c + 1]) for c in range(cols)]
    s[-1] = jnp.where(tail, s[-1], 0.0)

    r128, r_rem = power(7), power(8)
    closing, log_r = power(10), power(11)
    lane_f = lane.astype(jnp.float32)
    enter_west = jnp.exp(log_r * (lane_f + 1.0))
    enter_east = jnp.exp(log_r * (LANES - lane_f))
    enter_tail = jnp.exp(log_r * jnp.maximum(rem - lane_f, 0.0))
    stacked = jnp.concatenate(s, axis=0)
    high = stacked.astype(jnp.bfloat16)
    low = (stacked - high.astype(jnp.float32)).astype(jnp.bfloat16)
    product = jnp.dot(
        jnp.concatenate([high, low], axis=1), weights, preferred_element_type=jnp.float32
    )
    product = product[:, :LANES] + product[:, LANES:]
    y = [product[c * blocks : (c + 1) * blocks] for c in range(cols)]

    def spread(column, at):
        return jnp.broadcast_to(column[:, at : at + 1], (blocks, LANES))

    ends = [spread(y[c], LANES - 1 if c < cols - 1 else rem - 1) for c in range(cols)]
    begins = [spread(y[c], 0) for c in range(cols)]

    def closed(total, sign):
        total = pltpu.roll(total, 1 if sign > 0 else blocks - 1, 0)
        for k in range(blocks.bit_length() - 1):
            by = 1 << k
            total = total + power(12 + k) * pltpu.roll(total, by if sign > 0 else blocks - by, 0)
        return total * closing

    total = ends[0]
    for c in range(1, cols):
        total = ends[c] + (r128 if c < cols - 1 else r_rem) * total
    carry = closed(total, 1)
    for c in range(cols):
        y[c] = y[c] + enter_west * carry
        carry = ends[c] + r128 * carry
    total = begins[-1]
    for c in range(cols - 2, -1, -1):
        total = begins[c] + r128 * total
    carry = closed(total, -1)
    for c in range(cols - 1, -1, -1):
        y[c] = y[c] + (enter_tail if c == cols - 1 else enter_east) * carry
        carry = begins[c] + (r_rem if c == cols - 1 else r128) * carry
    filtered = jnp.full((blocks, LANES), marked, jnp.int32) == 1
    return [jnp.where(filtered, y[c], s[c]) for c in range(cols)]


def face_weights(plan, cy, t, row):
    last = plan.lat_total - 1
    c0 = jnp.where(row == 0, 0.0, cy[t, 0, row])
    c1 = jnp.where(row == last, 0.0, cy[t, 0, jnp.minimum(row + 1, last)])
    h0, h1 = 0.5 * (1.0 - c0), 0.5 * (1.0 - c1)
    return 1.0 - c1 * (1.0 + h1), c1 * h1 + c0 * (1.0 + h0), -c0 * h0


def start_all(copies):
    for copy in copies:
        copy.start()


def west_edge(plan, tail):
    return pltpu.roll(tail, LANES - plan.rem, tail.ndim - 1)


def east_edge(plan, first):
    return pltpu.roll(first, plan.rem, first.ndim - 1)


def zonal_taps(tiles, coef, lane, wanted):
    count = len(tiles)
    ahead = {}
    for c in range(max(min(wanted) - 1, 0), max(wanted) + 1):
        x = pltpu.roll(tiles[c], LANES - 2, 1)
        if c + 1 < count:
            x = jnp.where(lane >= LANES - 2, pltpu.roll(tiles[c + 1], LANES - 2, 1), x)
        u = jnp.where(coef[4] > 0.5, x, tiles[c])
        ahead[c] = [u] + [pltpu.roll(u, k, 1) for k in range(1, 4)]
    out = []
    for c in wanted:
        total = coef[0] * ahead[c][0]
        for k in range(1, 4):
            x = ahead[c][k]
            if c > 0:
                x = jnp.where(lane < k, ahead[c - 1][k], x)
            total = total + coef[k] * x
        out.append(total)
    return out


def kernel(plan, *refs):
    inputs, (x_ref, out_ref), tables, rest = refs[:5], refs[5:7], refs[7:15], refs[15:]
    cx, cy, shift, mask, table, cxv, shv, cyv = tables
    (x_local, x_sem, table_sem, packed, arrived, held, weights, ready, got, stage, got_south,
    f1_south, f1_out, ext, edge_out, edge_in, f1, taps, merid,
    in_send, in_recv, halo_send, halo_recv, own_in,
    south_in_send, south_in_recv, ext_send, ext_recv, f1_send, f1_recv, edge_send, edge_recv,
    out_send, out_recv, stage_recv, back_send, back_recv,
    south_out_send, south_out_recv, f2_send, f2_recv) = rest
    blocks, pitch, cols, lat, rem = plan.blocks, plan.pitch, plan.cols, plan.lat, plan.rem
    slots, bands, tiles, joint = plan.slots, plan.bands, plan.tiles, plan.joint
    unit_of = (plan.unit_a, plan.unit_h)
    me = lax.axis_index("lon")
    band = lax.axis_index("lat")
    low = band < 2
    polar = jnp.logical_or(band == 0, band == bands - 1)
    mid = jnp.logical_not(polar)
    helper = jnp.logical_or(band == 1, band == bands - 2)
    worker = jnp.logical_or(polar, helper)
    pole = jnp.where(low, 0, bands - 1)
    help_band = jnp.where(low, 1, bands - 2)
    mate = jnp.where(polar, help_band, pole)
    north_mid = jnp.logical_and(band >= 1, band < bands - 2)
    south_mid = jnp.logical_and(band >= 2, band < bands - 1)
    own = jnp.where(helper, plan.own_h, plan.own_a)
    count = jnp.where(helper, plan.groups_h, plan.groups_a)
    unit = jnp.where(helper, plan.unit_h, plan.unit_a)
    base = jnp.where(helper, plan.base_h, 0)

    def peer(k):
        return lax.rem(me + k, blocks)

    def at(lon, lat_at):
        return {"lon": lon, "lat": lat_at}

    barrier = pltpu.get_barrier_semaphore()

    def greet(lon, lat_at):
        pl.semaphore_signal(barrier, inc=1, device_id=at(lon, lat_at), device_id_type=MESH)

    @pl.when(worker)
    def _():
        for k in range(blocks):
            greet(peer(k), mate)
        for k in range(1, blocks):
            greet(peer(k), band)

    @pl.when(jnp.logical_not(worker))
    def _():
        greet(peer(1), band)
        greet(peer(blocks - 1), band)

    @pl.when(south_mid)
    def _():
        greet(me, band - 1)

    def lines(first, rows, wide=pitch):
        return pl.ds(pl.multiple_of(first * wide, 8), rows * wide)

    def load(f):
        part = pl.ds(f * lat, lat)
        return pltpu.make_async_copy(x_ref.at[part], x_local.at[part], x_sem.at[f])

    start_all([load(f) for f in range(plan.fields)])
    sources = inputs[:5] + (inputs[0], inputs[2], inputs[1])
    table_copies = [
        pltpu.make_async_copy(source, to, table_sem.at[i])
        for i, (source, to) in enumerate(zip(sources, tables))
    ]
    start_all(table_copies)
    packed[0 : HALO * pitch, :] = jnp.zeros((HALO * pitch, LANES), jnp.float32)
    lane = lax.broadcasted_iota(jnp.int32, (8, LANES), 1)
    sub = lax.broadcasted_iota(jnp.int32, (8, LANES), 0)

    def tile_of(part, c):
        width = LANES if c < cols - 1 else rem
        v = x_local[pl.ds(pl.multiple_of(part * 8, 8), 8), c * LANES : c * LANES + width]
        if width < LANES:
            v = jnp.concatenate([v, jnp.zeros((8, LANES - width), jnp.float32)], axis=1)
        return v

    def fill(part, none):
        for c in range(cols):
            packed[pl.ds((part * 8 + HALO) * pitch + c, 8, stride=pitch), :] = tile_of(part, c)
        return none

    def edges(part, none):
        rows = pl.ds(pl.multiple_of(part * 8, 8), 8)
        edge_out[0, rows, :] = west_edge(plan, tile_of(part, cols - 1))
        edge_out[1, rows, :] = east_edge(plan, tile_of(part, 0))
        return none

    for copy in table_copies:
        copy.wait()
    for f in range(plan.fields):
        load(f).wait()

    @pl.when(polar)
    def _():
        lax.fori_loop(0, plan.rows // 8, fill, 0)

    @pl.when(mid)
    def _():
        lax.fori_loop(0, plan.rows // 8, edges, 0, unroll=5)
        lax.fori_loop(0, plan.fields, lambda f, none: fill(f * tiles + tiles - 1, none), 0)

    row_id = lax.broadcasted_iota(jnp.int32, (8, plan.lat_total), 1)
    row_sub = lax.broadcasted_iota(jnp.int32, (8, plan.lat_total), 0)

    def rows_of(vector, first):
        hit = row_id == row_sub + first
        one = jnp.sum(jnp.where(hit, vector, 0.0), axis=1, keepdims=True)
        return jnp.broadcast_to(one, (8, LANES))

    for t in range(SUBS):
        for g in range(tiles):
            first = band * lat + g * 8
            c0 = jnp.where(sub + first == 0, 0.0, rows_of(cyv[t], first))
            c1 = rows_of(cyv[t], first + 1)
            h0, h1 = 0.5 * (1.0 - c0), 0.5 * (1.0 - c1)
            merid[t, g, 0] = 1.0 - c1 * (1.0 + h1)
            merid[t, g, 1] = c1 * h1 + c0 * (1.0 + h0)
            merid[t, g, 2] = -c0 * h0

    @pl.when(mid)
    def _():
        for t in range(SUBS):
            for g in range(tiles):
                first = band * lat + g * 8
                courant = rows_of(cxv[t], first)
                moved = rows_of(shv[t].astype(jnp.float32), first)
                half = 0.5 * (1.0 - courant)
                w0 = 1.0 - courant * (1.0 + half)
                w1 = courant * (1.0 + 2.0 * half)
                w2 = -courant * half
                ahead = moved < -0.5
                still = moved == jnp.where(ahead, -2.0, 0.0)
                taps[t, g, 0] = jnp.where(still, w0, 0.0)
                taps[t, g, 1] = jnp.where(still, w1, w0)
                taps[t, g, 2] = jnp.where(still, w2, w1)
                taps[t, g, 3] = jnp.where(still, 0.0, w2)
                taps[t, g, 4] = jnp.where(ahead, 1.0, 0.0)

    def place(slot):
        flat = base + me * own + slot - HALO
        south = slot >= slots - HALO
        row = jnp.where(south, slot - slots, lax.rem(flat + lat, lat))
        return south, jnp.maximum(pole * lat + row, 0)

    def build(i, none):
        for n in (2 * i, 2 * i + 1) if plan.joint == 2 else (i,):
            slot = jnp.where(n < own + HALO, n, n + slots - 2 * HALO - own)
            build_weights(table, place(slot)[1], weights, slot)
        return none

    @pl.when(polar)
    def _():
        lax.fori_loop(0, (own + 2 * HALO) // plan.joint, build, 0)

    def taps_of(t, i):
        g = lax.rem(i, tiles)
        return [taps[t, g, n] for n in range(TAPS)]

    def put(i, c, v):
        f1[i + i // tiles + 1, c * 8 : c * 8 + 8, :] = v

    def stepped(i, wanted):
        f, g = i // tiles, lax.rem(i, tiles)
        a = [merid[0, g, n] for n in range(3)]
        out = []
        for c in wanted:
            old = f1[i + f, c * 8 : c * 8 + 8, :]
            now = f1[i + f + 1, c * 8 : c * 8 + 8, :]
            one = jnp.where(sub < 1, pltpu.roll(old, 1, 0), pltpu.roll(now, 1, 0))
            two = jnp.where(sub < 2, pltpu.roll(old, 2, 0), pltpu.roll(now, 2, 0))
            out.append(a[0] * now + a[1] * one + a[2] * two)
        return out

    def keep(i, c, v):
        got[pl.ds(i * 8 * pitch + c, 8, stride=pitch), :] = v

    def first_inside(i, none):
        x = [tile_of(i, c) for c in range(cols)]
        for c, v in enumerate(zonal_taps(x, taps_of(0, i), lane, range(cols))):
            put(i, c + 1, v)
        return none

    def second_inside(i, none):
        x = stepped(i, range(1, cols + 1))
        inner = range(1, cols - 1)
        for c, v in zip(inner, zonal_taps(x, taps_of(1, i), lane, inner)):
            keep(i, c, v)
        return none

    def first_edges(i, none):
        rows = pl.ds(pl.multiple_of(i * 8, 8), 8)
        coef = taps_of(0, i)
        x = [edge_in[0, rows, :], tile_of(i, 0), tile_of(i, 1)]
        for c, v in enumerate(zonal_taps(x, coef, lane, range(2))):
            put(i, c, v)
        x = [tile_of(i, cols - 2), tile_of(i, cols - 1)]
        x[1] = jnp.where(lane < rem, x[1], edge_in[1, rows, :])
        put(i, cols, zonal_taps(x, coef, lane, [1])[0])
        return none

    def second_edges(i, none):
        coef = taps_of(1, i)
        keep(i, 0, zonal_taps(stepped(i, range(3)), coef, lane, [1])[0])
        keep(i, cols - 1, zonal_taps(stepped(i, [cols - 1, cols]), coef, lane, [1])[0])
        return none

    def northern(each, unroll):
        def at_tile(i, none):
            return each(i // (tiles - 1) * tiles + lax.rem(i, tiles - 1) + 1, none)

        lax.fori_loop(0, plan.fields * (tiles - 1), at_tile, 0, unroll=unroll)

    @pl.when(mid)
    def _():
        lax.fori_loop(0, plan.rows // 8, first_inside, 0, unroll=2)
        northern(second_inside, 3)

    pl.semaphore_wait(
        barrier,
        jnp.where(worker, 2 * blocks - 1, 2) + jnp.where(north_mid, 1, 0),
    )

    def remote(src, dst, send, recv, lon, lat_at):
        return pltpu.make_async_remote_copy(
            src_ref=src,
            dst_ref=dst,
            send_sem=send,
            recv_sem=recv,
            device_id=at(lon, lat_at),
            device_id_type=MESH,
        )

    def taken(ref, rows, sem, wide=pitch):
        part = ref.at[pl.ds(0, rows * wide)]
        pltpu.make_async_copy(part, part, sem).wait()

    def rows_in(role, k, g):
        own_r, first = (plan.own_h, plan.base_h) if role else (plan.own_a, 0)
        to = peer(k)
        step_rows = unit_of[role]
        return remote(
            packed.at[lines(HALO + first + to * own_r + g * step_rows, step_rows)],
            arrived.at[lines(me * slots + HALO + g * step_rows, step_rows)],
            in_send,
            in_recv.at[g],
            to,
            help_band if role else band,
        )

    def halo_in(role, k):
        own_r, first = (plan.own_h, plan.base_h) if role else (plan.own_a, 0)
        to = peer(k)
        return remote(
            packed.at[lines(first + to * own_r, HALO)],
            arrived.at[lines(me * slots, HALO)],
            halo_send,
            halo_recv,
            to,
            help_band if role else band,
        )

    own_copy = pltpu.make_async_copy(
        packed.at[lines(me * plan.own_a, plan.own_a + HALO)],
        arrived.at[lines(me * slots, plan.own_a + HALO)],
        own_in,
    )

    def start_in():
        for k in range(1, blocks):
            halo_in(0, k).start()
        for k in range(blocks):
            halo_in(1, k).start()
        for g in range(max(plan.groups_a, plan.groups_h)):
            for role in (1, 0):
                if g < (plan.groups_h if role else plan.groups_a):
                    for k in range(0 if role else 1, blocks):
                        rows_in(role, k, g).start()

    @pl.when(polar)
    def _():
        own_copy.start()
        start_in()

    def edge_copy(i):
        to = peer(1 if i == 0 else blocks - 1)
        return remote(edge_out.at[i], edge_in.at[i], edge_send.at[i], edge_recv.at[i], to, band)

    def south_parts(i):
        f, role, d = plan.south_to[i]
        src = packed.at[lines(HALO + f * lat + lat - HALO, HALO)]
        dst = arrived.at[lines(me * slots + slots - HALO, HALO)]
        return role, d, src, dst

    def south_in(i):
        role, d, src, dst = south_parts(i)
        return remote(
            src,
            dst,
            south_in_send.at[i],
            south_in_recv,
            jnp.int32(d),
            jnp.int32(bands - 2 if role else bands - 1),
        )

    def each_south_in(act, local):
        for i in range(len(plan.south_to)):
            role, d, src, dst = south_parts(i)
            if role:

                @pl.when(me != d)
                def _():
                    act(south_in(i))

                @pl.when(me == d)
                def _():
                    if local:
                        pltpu.make_async_copy(src, dst, south_in_recv).start()

            else:
                act(south_in(i))

    @pl.when(mid)
    def _():
        start_all([edge_copy(0), edge_copy(1)])

    @pl.when(band == bands - 2)
    def _():
        each_south_in(lambda copy: copy.start(), True)

    def show_north(f, none):
        for c in range(cols + 1):
            f1_out[pl.ds(f * HALO * plan.ext + c, HALO, stride=plan.ext), :] = f1[
                (f + 1) * (tiles + 1) - 1, c * 8 + 8 - HALO : c * 8 + 8, :
            ]
        return none

    f1_copy = remote(f1_out, f1_south, f1_send, f1_recv, me, band + 1)

    def f2_copy(f):
        return remote(
            got.at[lines(f * lat + lat - HALO, HALO)],
            got_south.at[lines(f * HALO, HALO)],
            f2_send,
            f2_recv,
            me,
            band + 1,
        )

    @pl.when(helper)
    def _():
        lax.fori_loop(0, (own + 2 * HALO) // plan.joint, build, 0)

    def close_first():
        for i in range(2):
            edge_copy(i).wait_recv()
        lax.fori_loop(0, plan.rows // 8, first_edges, 0, unroll=5)

        @pl.when(north_mid)
        def _():
            lax.fori_loop(0, plan.fields, show_north, 0, unroll=True)
            f1_copy.start()

    def close_second():
        northern(second_edges, 5)
        start_all([f2_copy(f) for f in range(plan.fields)])

    def steps(x, t, row, slot):
        return row_steps(
            plan,
            x,
            cx[t, 0, row],
            shift[t, 0, row],
            mask[row],
            lambda i: table[i, row],
            weights[slot],
        )

    def first_pass(slot):
        _, row = place(slot)
        x = [arrived[pl.ds(slot * pitch + c, blocks, stride=slots * pitch), :] for c in range(cols)]
        y = steps(x, 0, row, slot)
        for c in range(cols):
            held[slot, :, c * LANES : (c + 1) * LANES] = y[c]

    def second_pass(m):
        j = lax.rem(base + me * own + m, lat)
        row = pole * lat + j
        s0 = m + HALO
        s1 = jnp.where(j == 0, slots - 1, s0 - 1)
        s2 = jnp.where(j == 0, slots - 2, jnp.where(j == 1, slots - 1, s0 - 2))
        a0, a1, a2 = face_weights(plan, cy, 0, row)
        x = []
        for c in range(cols):
            part = slice(c * LANES, (c + 1) * LANES)
            x.append(a0 * held[s0, :, part] + a1 * held[s1, :, part] + a2 * held[s2, :, part])
        y = steps(x, 1, row, s0)
        for c in range(cols):
            ready[pl.ds(m * pitch + c, blocks, stride=plan.own_a * pitch), :] = y[c]

    def hosts(i):
        role, lon, _ = plan.piece(i)
        return jnp.logical_and(me == lon, band == role)

    def ext_parts(i, k):
        f, part = plan.pieces[i]
        src = ext.at[lines((part * blocks + peer(k)) * joint, joint, plan.ext)]
        return src, f1_south.at[lines(f * HALO + part * joint, joint, plan.ext)]

    def f2_parts(i, k):
        f, part = plan.pieces[i]
        src = ready.at[lines(peer(k) * plan.own_a + plan.piece(i)[2], joint)]
        return src, got_south.at[lines(f * HALO + part * joint, joint)]

    def piece_copies(i, parts, send, recv):
        helps = plan.piece(i)[0]
        return [
            remote(*parts(i, k), send.at[i], recv, peer(k), jnp.int32(1))
            for k in range(1 if helps else 0, blocks)
        ]

    def piece_start(i, parts, send, recv):
        start_all(piece_copies(i, parts, send, recv))
        if plan.piece(i)[0]:
            pltpu.make_async_copy(*parts(i, 0), recv).start()

    wide_lane = lax.broadcasted_iota(jnp.int32, (blocks, LANES), 1)

    def widen(i):
        _, _, inside = plan.piece(i)
        part = plan.pieces[i][1]
        for u in range(joint):
            x = [held[inside + u + HALO, :, c * LANES : (c + 1) * LANES] for c in range(cols)]
            west = west_edge(plan, pltpu.roll(x[-1], 1, 0))
            east = east_edge(plan, pltpu.roll(x[0], blocks - 1, 0))
            x[-1] = jnp.where(wide_lane < rem, x[-1], east)
            for c, v in enumerate([west] + x):
                first = (part * blocks * joint + u) * plan.ext + c
                ext[pl.ds(first, blocks, stride=joint * plan.ext), :] = v

    def each_row(g, do):
        def some(i, none):
            for u in range(joint):
                do(g * unit + i * joint + u)
            return none

        lax.fori_loop(0, unit // joint, some, 0)

    def first_group(g):
        @pl.when(polar)
        def _():
            taken(arrived, (blocks - 1) * plan.unit_a, in_recv.at[g])

        @pl.when(helper)
        def _():
            taken(arrived, blocks * plan.unit_h, in_recv.at[g])

        each_row(g, lambda m: first_pass(m + HALO))
        for i in range(len(plan.pieces)):

            @pl.when(jnp.logical_and(hosts(i), g == plan.piece(i)[2] // unit_of[plan.piece(i)[0]]))
            def _():
                widen(i)
                piece_start(i, ext_parts, ext_send, ext_recv)

    is_host = False
    for _, role, d in plan.south_to:
        its = bands - 2 if role else bands - 1
        is_host = jnp.logical_or(is_host, jnp.logical_and(me == d, band == its))

    def others():
        @pl.when(polar)
        def _():
            taken(arrived, (blocks - 1) * HALO, halo_recv)

        @pl.when(helper)
        def _():
            taken(arrived, blocks * HALO, halo_recv)

        @pl.when(is_host)
        def _():
            taken(arrived, blocks * HALO, south_in_recv)

        def two(i, none):
            for u in range(HALO):
                first_pass(i * (slots - HALO) + u)
            return none

        lax.fori_loop(0, 1 + jnp.where(is_host, 1, 0), two, 0)

    def own_back(g):
        rows = plan.unit_a
        part = pl.multiple_of((me * plan.own_a + g * rows) * pitch, 8)
        part = pl.ds(part, rows * pitch)
        return pltpu.make_async_copy(ready.at[part], got.at[part], out_recv)

    def own_stage(g):
        rows = plan.unit_h
        return pltpu.make_async_copy(
            ready.at[lines(me * plan.own_a + g * rows, rows)],
            stage.at[lines(me * plan.own_h + g * rows, rows)],
            stage_recv.at[g],
        )

    def rows_out(k, g):
        rows = plan.unit_a
        return remote(
            ready.at[lines(peer(k) * plan.own_a + g * rows, rows)],
            got.at[lines(me * plan.own_a + g * rows, rows)],
            out_send,
            out_recv,
            peer(k),
            band,
        )

    def rows_home(k, g):
        rows = plan.unit_h
        return remote(
            ready.at[lines(peer(k) * plan.own_a + g * rows, rows)],
            got.at[lines(plan.base_h + me * plan.own_h + g * rows, rows)],
            out_send,
            back_recv,
            peer(k),
            mate,
        )

    def rows_stage(k, g):
        rows = plan.unit_h
        return remote(
            ready.at[lines(peer(k) * plan.own_a + g * rows, rows)],
            stage.at[lines(me * plan.own_h + g * rows, rows)],
            out_send,
            stage_recv.at[g],
            peer(k),
            band,
        )

    def relay(g):
        taken(stage, blocks * plan.unit_h, stage_recv.at[g])
        wide = plan.own_h * pitch
        part = pl.ds(pl.multiple_of(g * plan.unit_h * pitch, 8), plan.unit_h * pitch)
        landing = got.at[pl.ds(plan.base_h * pitch, blocks * wide)]
        remote(
            stage.reshape(blocks, wide, LANES).at[:, part, :],
            landing.reshape(blocks, wide, LANES).at[:, part, :],
            back_send,
            back_recv,
            me,
            mate,
        ).start()

    def ship(g):
        @pl.when(polar)
        def _():
            start_all([rows_out(k, g) for k in range(1, blocks)])
            own_back(g).start()

        @pl.when(helper)
        def _():
            @pl.when(g < plan.relayed)
            def _():
                start_all([rows_stage(k, g) for k in range(1, blocks)])
                own_stage(g).start()

            @pl.when(g >= plan.relayed)
            def _():
                start_all([rows_home(k, g) for k in range(blocks)])

        for i in range(len(plan.pieces)):

            @pl.when(jnp.logical_and(hosts(i), g == plan.piece(i)[2] // unit_of[plan.piece(i)[0]]))
            def _():
                piece_start(i, f2_parts, south_out_send, south_out_recv)

    @pl.when(polar)
    def _():
        own_copy.wait()

    @pl.when(jnp.logical_and(worker, low))
    def _():
        held[slots - HALO :, :, :] = jnp.zeros((HALO, blocks, cols * LANES), jnp.float32)

    def step(s, none):
        first_group(s)
        each_row(s, second_pass)
        ship(s)

        @pl.when(jnp.logical_and(helper, s == 0))
        def _():
            close_first()

        @pl.when(jnp.logical_and(helper, s == min(1, plan.groups_h - 1)))
        def _():
            close_second()

        @pl.when(jnp.logical_and(helper, jnp.logical_and(s >= plan.lag, s < plan.relayed + plan.lag)))
        def _():
            relay(s - plan.lag)

        return none

    if bands > 4:

        @pl.when(jnp.logical_not(worker))
        def _():
            close_first()
            close_second()

    @pl.when(worker)
    def _():
        others()
        lax.fori_loop(0, count, step, 0)

        @pl.when(helper)
        def _():
            for g in range(max(plan.groups_h - plan.lag, 0), plan.relayed):
                relay(g)

    @pl.when(band == 1)
    def _():
        taken(f1_south, plan.fields * HALO, ext_recv, plan.ext)

    @pl.when(south_mid)
    def _():
        remote(f1_out, f1_south, f1_send, f1_recv, me, band + 1).wait_recv()

    @pl.when(mid)
    def _():
        def outer(f, none):
            for c in range(cols + 1):
                f1[f * (tiles + 1), c * 8 + 8 - HALO : c * 8 + 8, :] = f1_south[
                    pl.ds(f * HALO * plan.ext + c, HALO, stride=plan.ext), :
                ]
            i = f * tiles
            x = stepped(i, range(cols + 1))
            for c, v in enumerate(zonal_taps(x, taps_of(1, i), lane, range(1, cols + 1))):
                keep(i, c, v)
            return none

        lax.fori_loop(0, plan.fields, outer, 0)

    @pl.when(polar)
    def _():
        taken(got, plan.base_h, out_recv)

    @pl.when(band == 0)
    def _():
        got_south[...] = jnp.zeros_like(got_south)

    @pl.when(band == 1)
    def _():
        taken(got_south, plan.fields * HALO, south_out_recv)

    @pl.when(band >= 2)
    def _():
        taken(got_south, plan.fields * HALO, f2_recv)

    def one_field(f, none):
        for g in range(tiles):
            a0, a1, a2 = (merid[SUBS - 1, g, i] for i in range(3))
            for c in range(cols):
                first = (f * lat + g * 8) * pitch + c
                x0 = got[pl.ds(first, 8, stride=pitch), :]
                if g:
                    x1 = got[pl.ds(first - pitch, 8, stride=pitch), :]
                    x2 = got[pl.ds(first - 2 * pitch, 8, stride=pitch), :]
                else:
                    south2 = got_south[pl.ds(f * HALO * pitch + c, 1), :]
                    south1 = got_south[pl.ds((f * HALO + 1) * pitch + c, 1), :]
                    x1 = jnp.where(sub == 0, south1, pltpu.roll(x0, 1, 0))
                    x2 = jnp.where(
                        sub == 0, south2, jnp.where(sub == 1, south1, pltpu.roll(x0, 2, 0))
                    )
                v = a0 * x0 + a1 * x1 + a2 * x2
                width = LANES if c < cols - 1 else rem
                out_ref[f, 0, g * 8 : g * 8 + 8, c * LANES : c * LANES + width] = v[:, :width]
        return none

    early = plan.base_h // lat
    lax.fori_loop(0, early, one_field, 0)

    @pl.when(polar)
    def _():
        taken(got, plan.rows - plan.base_h, back_recv)

    lax.fori_loop(early, plan.fields, one_field, 0, unroll=True)

    @pl.when(polar)
    def _():
        taken(packed, (blocks - 1) * plan.own_a + blocks * plan.own_h, in_send)
        taken(ready, (blocks - 1) * plan.own_a, out_send)

        taken(packed, (2 * blocks - 1) * HALO, halo_send)

    @pl.when(helper)
    def _():
        straight = plan.own_h - plan.relayed * plan.unit_h
        taken(ready, (blocks - 1) * plan.own_h + straight, out_send)
        if plan.relayed:
            taken(stage, blocks * plan.relayed * plan.unit_h, back_send)

    for i in range(len(plan.pieces)):

        @pl.when(hosts(i))
        def _():
            sent = blocks - plan.piece(i)[0]
            taken(ext, sent * joint, ext_send.at[i], plan.ext)
            taken(ready, sent * joint, south_out_send.at[i])

    @pl.when(band == bands - 2)
    def _():
        each_south_in(lambda copy: copy.wait_send(), False)

    @pl.when(north_mid)
    def _():
        f1_copy.wait_send()

    @pl.when(mid)
    def _():
        for i in range(2):
            edge_copy(i).wait_send()
        taken(got, plan.fields * HALO, f2_send)


def body(plan, fields, frac_x, frac_y, shift_cells, polar_mask):
    blocks, pitch = plan.blocks, plan.pitch
    anywhere = pl.BlockSpec(memory_space=pltpu.HBM)
    dma = pltpu.SemaphoreType.DMA
    n_pieces = len(plan.pieces)

    def lines(rows, wide=pitch):
        return pltpu.VMEM((rows * wide, LANES), jnp.float32)

    tables = (frac_x, frac_y, shift_cells, polar_mask, jnp.asarray(decay_table(plan)))
    edge = pltpu.VMEM((2, plan.rows, LANES), jnp.float32)
    return pl.pallas_call(
        functools.partial(kernel, plan),
        out_shape=pltpu.VMEM(fields.shape, jnp.float32),
        in_specs=[anywhere] * 6,
        out_specs=pl.BlockSpec(memory_space=pltpu.VMEM),
        scratch_shapes=[
            *[pltpu.SMEM(table.shape, table.dtype) for table in tables],
            *[pltpu.VMEM(tables[i].shape, tables[i].dtype) for i in (0, 2, 1)],
            pltpu.VMEM((plan.rows, plan.lon), jnp.float32),
            dma((plan.fields,)),
            dma((len(tables) + 3,)),
            lines(HALO + plan.rows),
            lines(blocks * plan.slots),
            pltpu.VMEM((plan.slots, blocks, plan.cols * LANES), jnp.float32),
            pltpu.VMEM((plan.slots, 2 * LANES, 2 * LANES), jnp.bfloat16),
            lines(blocks * plan.own_a),
            lines(plan.rows),
            lines(blocks * plan.own_h),
            lines(plan.fields * HALO),
            lines(plan.fields * HALO, plan.ext),
            lines(plan.fields * HALO, plan.ext),
            lines(blocks * HALO, plan.ext),
            edge,
            edge,
            pltpu.VMEM((plan.fields * (plan.tiles + 1), 8 * (plan.cols + 1), LANES), jnp.float32),
            pltpu.VMEM((SUBS, plan.tiles, TAPS, 8, LANES), jnp.float32),
            pltpu.VMEM((SUBS, plan.tiles, 3, 8, LANES), jnp.float32),
            dma,
            dma((max(plan.groups_a, plan.groups_h),)),
            dma,
            dma,
            dma,
            dma((len(plan.south_to),)),
            dma,
            dma((n_pieces,)),
            dma,
            dma,
            dma,
            dma((2,)),
            dma((2,)),
            dma,
            dma,
            dma((plan.groups_h,)),
            dma,
            dma,
            dma((n_pieces,)),
            dma,
            dma,
            dma,
        ],
        compiler_params=pltpu.CompilerParams(
            collective_id=0, has_side_effects=True, vmem_limit_bytes=VMEM_LIMIT
        ),
        name="transport",
    )(
        *tables,
        fields.reshape(plan.rows, plan.lon),
    )


def solution(mesh):
    def whole(fields, frac_x, frac_y, shift_cells, polar_mask):
        return jax.shard_map(
            functools.partial(body, Plan(mesh, fields.shape)),
            mesh=mesh,
            in_specs=(P(None, None, "lat", "lon"), P(), P(), P(), P()),
            out_specs=P(None, None, "lat", "lon"),
            check_vma=False,
        )(fields, frac_x, frac_y, shift_cells, polar_mask)

    return whole
```
